128 devices in a mesh: seq: 32 (over z_hi, y, x), head: 4 (over z_lo, core).
Axes of the slice: x: 4, y: 4, z: 4 (z_hi: 2, z_lo: 2; z = z_hi * 2 + z_lo), core: 2. Of those that a mesh axis runs over, the one named last changes fastest.
Arguments:
- x_in: bfloat16 [16384, 4096], P('seq', 'head'), may hold values from -6 to 6
- z_in: bfloat16 [16384, 4096], P('seq', 'head'), may hold values from -6 to 6
- b_in: bfloat16 [16384, 512], P('seq', 'head'), may hold values from -0.5 to 0.5
- c_in: bfloat16 [16384, 512], P('seq', 'head'), may hold values from -0.5 to 0.5
- dt_raw: float32 [64, 16384], P('head', 'seq')
- dt_bias: float32 [64], P('head'), may hold values from -5 to -4
- a_log: float32 [64], P('head')
- d_skip: float32 [64], P('head'), may hold values from 0.1 to 1.9
- gain: float32 [4096], P('head'), may hold values from 0.5 to 1.5
- resets: int32 [64, 128], P('head', 'seq'), may hold values 0 or 1
- out_weight: bfloat16 [4096, 4096], P('seq', 'head'), may hold values from -0.09375 to 0.09375
- cotangent: bfloat16 [16384, 4096], P('seq', 'head'), may hold values from -6 to 6
Outputs:
- d_x: bfloat16 [16384, 4096], P('seq', 'head')
- d_z: bfloat16 [16384, 4096], P('seq', 'head')
- d_b: bfloat16 [16384, 512], P('seq', 'head')
- d_c: bfloat16 [16384, 512], P('seq', 'head')
- raw_timestep_gradient: float32 [64, 16384], P('head', 'seq')
- d_out_weight: float32 [4096, 4096], P('seq', 'head')
The draws below stay inside these ranges and needn't reach their ends.
All inputs are finite; a program needn't handle non-finite values. No bound on the sum of `resets` on one device may be relied on, other than what follows from the above.
Results may differ from the reference program's by a relative error of at most 0.0075.
Values may be sent and summed in bfloat16 or wider, within the bound.
A program may use at most 256 MiB of HBM per device.

```python
from functools import partial
import jax
import jax.numpy as jnp
from jax import lax

D = 4096
MIXER_HEADS = 64
HEADDIM = 64
STATE = 128
GROUPS = 4
BLOCK = 128
TOK_DEV = 512
INNER = 4096
SEQUENCE_LENGTH = 16384
NBLOCKS = 128


def draw_a_log(key, part):
    picker, levels = jax.random.split(jax.random.fold_in(key, 11))
    share = 0.5
    slow = jax.random.uniform(picker, (MIXER_HEADS,)) < share
    unit = jax.random.uniform(levels, (MIXER_HEADS,), dtype=jnp.float32)
    slow_value = jnp.log(40.0 / SEQUENCE_LENGTH) + unit * jnp.log(3.0)
    fast_value = jnp.log(1.5) + unit * jnp.log(2.0)
    return jnp.where(slow, slow_value, fast_value).astype(jnp.float32)


def draw_dt_raw(key, part):
    first, second, third_piece = jax.random.split(jax.random.fold_in(key, 23), 3)
    start_offsets = jax.random.uniform(first, (MIXER_HEADS, SEQUENCE_LENGTH // TOK_DEV, 1), minval=-0.7, maxval=0.7)
    start_offsets = jnp.broadcast_to(start_offsets, (MIXER_HEADS, SEQUENCE_LENGTH // TOK_DEV, TOK_DEV)).reshape(MIXER_HEADS, SEQUENCE_LENGTH)
    random_jitter = 0.4 * jax.random.normal(second, (MIXER_HEADS, SEQUENCE_LENGTH))
    document_runs = jax.random.uniform(third_piece, (MIXER_HEADS, SEQUENCE_LENGTH)) < 3.0 / SEQUENCE_LENGTH
    return (start_offsets + random_jitter + jnp.where(document_runs, 150.0, 0.0)).astype(jnp.float32)


def set_ends(drawn, stream_key, smallest, high):
    extent = drawn.shape
    index_at = [jax.random.randint(jax.random.fold_in(stream_key, axis), (), 0, extent[axis]) for axis in range(len(extent))]
    drawn = drawn.at[tuple(index_at)].set(smallest)
    longest = extent.index(max(extent))
    index_at[longest] = (index_at[longest] + 1) % extent[longest]
    return drawn.at[tuple(index_at)].set(high)


def raised(values, stream_key, source, target, shards_of, factor):
    owner, partner = [(jnp.arange(values.shape[dim]) // (values.shape[dim] // shards_of)).reshape([-1 if axis == dim else 1 for axis in range(values.ndim)]) for dim in (source, target)]
    chosen = jax.random.permutation(stream_key, shards_of)[partner]
    strong = (owner == chosen) | (owner == (partner + shards_of // 2) % shards_of)
    return jnp.where(strong, factor * values, values)


def shard_levels(rng, dims, cuts, low, largest):
    def one(dim, shards_of):
        heights = jax.random.uniform(jax.random.fold_in(jax.random.fold_in(rng, 6), dim), (shards_of,), jnp.float32, low / len(cuts), largest / len(cuts))
        return jnp.repeat(jnp.exp(heights), dims[dim] // shards_of).reshape((-1,) + (1,) * (len(dims) - dim - 1))

    factor_of = one(*cuts[0])
    for cut in cuts[1:]:
        factor_of = factor_of * one(*cut)
    return factor_of


def bell_draw(stream_key, shape, deviation, most, pieces=(), kind=jnp.bfloat16):
    loudness = shard_levels(stream_key, shape, pieces, -0.22, 0.18) if pieces else 1.0
    entries = jax.random.normal(stream_key, shape, jnp.float32) * deviation * loudness
    return jnp.minimum(jnp.maximum(entries, -most), most).astype(kind)


def heavy_noise(own_key, dims, scale, most, pieces, heavy, kind=jnp.bfloat16):
    array = scale * jax.random.normal(own_key, dims, jnp.float32)
    if pieces:
        array = array * shard_levels(own_key, dims, pieces, -0.22, 0.18)
    return jnp.clip(raised(array, jax.random.fold_in(own_key, 3), *heavy), -most, most).astype(kind)


def setup_inputs(seed: int = 0) -> dict:
    keys = jax.random.split(jax.random.key(seed), 13)
    x_in = bell_draw(keys[0], (SEQUENCE_LENGTH, INNER), 1.0, 6.0, ((0, 32), (1, 4)))
    z_in = bell_draw(keys[1], (SEQUENCE_LENGTH, INNER), 1.0, 6.0, ((0, 32), (1, 4)))
    b_in = bell_draw(keys[2], (SEQUENCE_LENGTH, GROUPS * STATE), STATE ** -0.5, 0.5, ((0, 32), (1, 4)))
    c_in = bell_draw(keys[3], (SEQUENCE_LENGTH, GROUPS * STATE), STATE ** -0.5, 0.5, ((0, 32), (1, 4)))
    dt_raw = draw_dt_raw(jax.random.fold_in(keys[12], 71), 0)
    dt_bias = jnp.clip(-5.0 + 1.0 * jax.random.uniform(keys[5], (MIXER_HEADS,), jnp.float32) ** shard_levels(keys[5], (MIXER_HEADS,), ((0, 4),), -0.2, 0.2), -5.0, -4.0)
    a_log = draw_a_log(jax.random.fold_in(keys[12], 71), 0)
    d_skip = jnp.clip(1.0 + 0.18 * jax.random.normal(keys[7], (MIXER_HEADS,), jnp.float32), 0.1, 1.9)
    gain = jnp.clip(1.0 + 0.1 * jax.random.normal(keys[8], (INNER,), jnp.float32), 0.5, 1.5)
    resets = set_ends((jax.random.randint(keys[9], (MIXER_HEADS, NBLOCKS), 0, 64) < 1).astype(jnp.int32), jax.random.fold_in(keys[9], 1), 0, 1)
    out_weight = bell_draw(keys[10], (D, INNER), INNER ** -0.5, 0.09375, ((0, 32), (1, 4)))
    cotangent = heavy_noise(keys[11], (SEQUENCE_LENGTH, D), 1.0, 6.0, ((0, 32), (1, 4)), (0, 1, 32, 2.75))
    return {"x_in": x_in, "z_in": z_in, "b_in": b_in, "c_in": c_in, "dt_raw": dt_raw, "dt_bias": dt_bias, "a_log": a_log, "d_skip": d_skip, "gain": gain, "resets": resets, "out_weight": out_weight, "cotangent": cotangent}


highest = lax.Precision.HIGHEST

def block_step(state, inputs, per_group, skip_gain):
    x_block, b_block, c_block, rate_block, step_block, keep_block = inputs
    running = jnp.cumsum(rate_block, axis=1)
    positions = rate_block.shape[1]
    lower = jnp.arange(positions)[:, None] >= jnp.arange(positions)[None, :]
    spread = jnp.where(lower[None], running[:, :, None] - running[:, None, :], 0.0)
    decays = jnp.exp(spread) * lower[None].astype(jnp.float32)
    scores = jnp.einsum('tgn,sgn->gts', c_block, b_block, precision=highest)
    scores = jnp.repeat(scores, per_group, axis=0)
    mixing = scores * decays * step_block[:, None, :]
    within = jnp.einsum('hts,shp->thp', mixing, x_block, precision=highest)
    c_heads = jnp.repeat(c_block, per_group, axis=1)
    b_heads = jnp.repeat(b_block, per_group, axis=1)
    carried = state * keep_block[:, None, None]
    incoming = jnp.einsum('thn,hpn->thp', c_heads, carried, precision=highest) * jnp.exp(running).T[:, :, None]
    output = within + incoming + skip_gain[None, :, None] * x_block
    weighted = (jnp.exp(running[:, -1:] - running) * step_block).T
    fresh = jnp.einsum('sh,shp,shn->hpn', weighted, x_block, b_heads, precision=highest)
    return (carried * jnp.exp(running[:, -1])[:, None, None] + fresh, output)

def scan_blocks(inputs, bmatrix, cmatrix, dt_raw, start, dt_bias, a_log, d_skip, keep):
    positions = inputs.shape[0]
    heads = dt_raw.shape[0]
    groups = bmatrix.shape[1] // STATE
    blocks = positions // BLOCK
    step_size = jax.nn.softplus(dt_raw + dt_bias[:, None])
    rate = -step_size * jnp.exp(a_log)[:, None]
    x_blocks = inputs.reshape(blocks, BLOCK, heads, HEADDIM)
    b_blocks = bmatrix.reshape(blocks, BLOCK, groups, STATE)
    c_blocks = cmatrix.reshape(blocks, BLOCK, groups, STATE)
    rate_blocks = rate.reshape(heads, blocks, BLOCK).transpose(1, 0, 2)
    step_blocks = step_size.reshape(heads, blocks, BLOCK).transpose(1, 0, 2)
    stepper = partial(block_step, per_group=heads // groups, skip_gain=d_skip)
    final, outputs = lax.scan(stepper, start, (x_blocks, b_blocks, c_blocks, rate_blocks, step_blocks, keep.T))
    return (outputs.reshape(positions, heads * HEADDIM), final)

def gate_norm(mixed, gates, gain, groups):
    gated = mixed * jax.nn.silu(gates)
    count = gated.shape[0]
    grouped = gated.reshape(count, groups, -1)
    factor = lax.rsqrt(lax.optimization_barrier(jnp.mean(grouped * grouped, axis=2, keepdims=True)) + 1e-05)
    return (grouped * factor).reshape(count, -1) * gain

def reference(x_in, z_in, b_in, c_in, dt_raw, dt_bias, a_log, d_skip, gain, resets, out_weight, cotangent):
    keep = 1.0 - resets.astype(jnp.float32)
    zero_state = jnp.zeros((MIXER_HEADS, HEADDIM, STATE), jnp.float32)

    def forward(x_wide, input_matrix_wide, c_wide, raw_steps, z_wide):
        mixed, final = scan_blocks(x_wide, input_matrix_wide, c_wide, raw_steps, zero_state, dt_bias, a_log, d_skip, keep)
        return gate_norm(mixed, z_wide, gain, GROUPS)
    normed, pullback = jax.vjp(forward, x_in.astype(jnp.float32), b_in.astype(jnp.float32), c_in.astype(jnp.float32), dt_raw, z_in.astype(jnp.float32))
    normed_half = normed.astype(jnp.bfloat16)
    d_normed = jnp.dot(cotangent, out_weight, preferred_element_type=jnp.float32)
    grad_x, grad_b, grad_c, grad_steps, grad_z = pullback(d_normed)
    d_out_weight = jnp.dot(cotangent.T, normed_half, preferred_element_type=jnp.float32)
    return (grad_x.astype(jnp.bfloat16), grad_z.astype(jnp.bfloat16), grad_b.astype(jnp.bfloat16), grad_c.astype(jnp.bfloat16), grad_steps, d_out_weight)
```

```python
import functools

import jax
import jax.numpy as jnp
from jax import lax
from jax.experimental import pallas as pl
from jax.experimental.pallas import tpu as pltpu
from jax.sharding import PartitionSpec as P

T = 512
N = 128
HP = 1024
H = 16
NB = T // N
NP = HP // N
SEQ = 32

f32 = jnp.float32
bf16 = jnp.bfloat16
HI = lax.Precision.HIGHEST
NN = (((1,), (0,)), ((), ()))
NT = (((1,), (1,)), ((), ()))
TN = (((0,), (0,)), ((), ()))
OFF = -1e30


def dot(a, b, dims=NN, precision=None):
    return lax.dot_general(a, b, dims, precision=precision, preferred_element_type=f32)


def iota(shape, axis):
    return lax.broadcasted_iota(jnp.int32, shape, axis)


def pair_of(ref, rows, j, count):
    first = jnp.broadcast_to(ref[rows, 2 * j : 2 * j + 1], (count, N))
    second = jnp.broadcast_to(ref[rows, 2 * j + 1 : 2 * j + 2], (count, N))
    return jnp.where(iota((count, N), 1) < 64, first, second), first, second


def head_rows():
    row, col = iota((H, HP), 0), iota((H, HP), 1)
    return ((col >= 64 * row) & (col < 64 * row + 64)).astype(bf16)


def halves(value):
    high = value.astype(bf16)
    return high, (value - high.astype(f32)).astype(bf16)


def head_sums(value):
    high, low = halves(value)
    ones = head_rows()
    return dot(ones, high, NT) + dot(ones, low, NT)


def stacked(value):
    low = iota(value.shape, 1) < 64
    zero = jnp.zeros_like(value)
    return jnp.concatenate([jnp.where(low, value, zero), jnp.where(low, zero, value)], axis=0)


def lanes(j):
    return slice(N * j, N * j + N)


def prepare(dt, bias, alog, step, r, step_t, r_t):
    raw = dt[...] + bias[...]
    step[...] = jnp.maximum(raw, 0.0) + jnp.log1p(jnp.exp(-jnp.abs(raw)))
    rate = -step[...] * jnp.exp(alog[...])
    row, col = iota((N, N), 0), iota((N, N), 1)
    upper = (row <= col).astype(f32)
    eye = (row == col).astype(f32)
    for b in range(NB):
        at = lanes(b)
        r[:, at] = dot(rate[:, at], upper, precision=HI)
        r_t[at, :] = dot(eye, r[:, at], NT, HI)
        step_t[at, :] = dot(eye, step[:, at], NT, HI)


def forward_block(b, x, bm, cm, r, r_t, step_t, keep_t, within, er, xw, sl, pd, st):
    base = pl.multiple_of(b * N, N)
    rows = pl.ds(base, N)
    mask = iota((N, N), 0) >= iota((N, N), 1)
    b_blk, c_blk = bm[rows, :], cm[rows, :]
    b_flip = b_blk.astype(f32).T.astype(bf16)
    scores = dot(c_blk, b_blk, NT)
    for j in range(NP):
        at = lanes(j)
        run, run0, run1 = pair_of(r_t, rows, j, N)
        size = pair_of(step_t, rows, j, N)[0]
        last = pair_of(r_t, pl.ds(base + N - 1, 1), j, 1)[0]
        keep = pair_of(keep_t.at[b], slice(0, 1), j, 1)[0]
        mixing = [
            (jnp.exp(jnp.where(mask, col - r[2 * j + k : 2 * j + k + 1, rows], OFF)) * scores).astype(bf16)
            for k, col in enumerate((run0, run1))
        ]
        x_val = x[rows, at].astype(f32)
        sized = x_val * size
        within[rows, at] = dot(jnp.concatenate(mixing, axis=1), stacked(sized.astype(bf16)))
        er[rows, at] = jnp.exp(run)
        weighted = (sized * jnp.exp(last - run)).astype(bf16)
        xw[rows, at] = weighted
        state = st[:, at] * keep
        sl[b, :, at] = state
        span = pd[b, :, at] * keep
        pd[b, :, at] = span
        decay = jnp.exp(last)
        pd[b + 1, :, at] = span * decay
        st[:, at] = state * decay + dot(b_flip, weighted)


def forward_local(*refs):
    sl, pd, st = refs[-3:]
    st[...] = jnp.zeros_like(st)
    pd[0] = jnp.ones((1, HP), f32)

    def step(b, carry):
        forward_block(b, *refs)
        return carry

    lax.fori_loop(0, NB, step, 0)
    sl[NB] = st[...]


def enter(x, cm, sl, pd, entering, er, skip, within, y, sin):
    def step(b, carry):
        rows = pl.ds(pl.multiple_of(b * N, N), N)
        c_blk = cm[rows, :]
        for j in range(NP):
            at = lanes(j)
            state = sl[b, :, at] + pd[b, :, at] * entering[:, at]
            sin[b, :, at] = state
            high, low = halves(state)
            y[rows, at] = within[rows, at] + (dot(c_blk, high) + dot(c_blk, low)) * er[rows, at] + skip[:, at] * x[rows, at].astype(f32)
        return carry

    lax.fori_loop(0, NB, step, 0)


CH = 32


def norm(y, z, gain, normed):
    def step(i, carry):
        rows = pl.ds(pl.multiple_of(i * CH, CH), CH)
        z_val = z[rows, :].astype(f32)
        gated = y[rows, :] * (z_val / (1.0 + jnp.exp(-z_val)))
        factor = lax.rsqrt(jnp.mean(gated * gated, axis=1, keepdims=True) + 1e-05)
        normed[rows, :] = (gated * factor * gain[...]).astype(bf16)
        return carry

    lax.fori_loop(0, T // CH, step, 0)


def unnorm(y, within, x, z, gain, skip, d_normed, d_z, d_y, work, carried):
    def step(i, carry):
        rows = pl.ds(pl.multiple_of(i * CH, CH), CH)
        z_val = z[rows, :].astype(f32)
        y_val = y[rows, :]
        sig = 1.0 / (1.0 + jnp.exp(-z_val))
        silu = z_val * sig
        gated = y_val * silu
        factor = lax.rsqrt(jnp.mean(gated * gated, axis=1, keepdims=True) + 1e-05)
        scaled = d_normed[rows, :] * gain[...]
        along = jnp.mean(scaled * gated, axis=1, keepdims=True)
        d_gated = factor * scaled - gated * (factor * factor * factor * along)
        d_z[rows, :] = (d_gated * y_val * (sig * (1.0 + z_val * (1.0 - sig)))).astype(bf16)
        d_mixed = d_gated * silu
        d_y[rows, :] = d_mixed
        own = within[rows, :]
        work[rows, :] = d_mixed * own
        carried[rows, :] = d_mixed * (y_val - skip[...] * x[rows, :].astype(f32) - own)
        return carry

    lax.fori_loop(0, T // CH, step, 0)


def gather_heads(work, sums):
    def step(b, carry):
        rows = pl.ds(pl.multiple_of(b * N, N), N)
        sums[:, rows] = head_sums(work[rows, :])
        return carry

    lax.fori_loop(0, NB, step, 0)


def state_grad(cm, r_t, keep_t, er, d_y, erdy, gl, qd, gt):
    gt[...] = jnp.zeros_like(gt)
    qd[NB - 1] = jnp.ones((1, HP), f32)

    def step(i, carry):
        b = NB - 1 - i
        base = pl.multiple_of(b * N, N)
        rows = pl.ds(base, N)
        c_flip = cm[rows, :].astype(f32).T.astype(bf16)
        for j in range(NP):
            at = lanes(j)
            last = pair_of(r_t, pl.ds(base + N - 1, 1), j, 1)[0]
            keep = pair_of(keep_t.at[b], slice(0, 1), j, 1)[0]
            high, low = halves(er[rows, at] * d_y[rows, at])
            erdy[0, rows, at] = high
            erdy[1, rows, at] = low
            grad = gt[:, at]
            gl[b, :, at] = grad
            decay = jnp.exp(last)
            gt[:, at] = keep * (decay * grad + dot(c_flip, high) + dot(c_flip, low))
            value = qd[b, :, at]

            @pl.when(b > 0)
            def _():
                qd[b - 1, :, at] = keep * decay * value

        return carry

    lax.fori_loop(0, NB, step, 0)


def backward_within(x, bm, cm, r, r_t, step_t, d_y, v, ds):
    def step(b, carry):
        rows = pl.ds(pl.multiple_of(b * N, N), N)
        mask = iota((N, N), 0) <= iota((N, N), 1)
        scores = dot(bm[rows, :], cm[rows, :], NT)
        total = jnp.zeros((N, N), f32)
        for j in range(NP):
            at = lanes(j)
            run0 = jnp.broadcast_to(r_t[rows, 2 * j : 2 * j + 1], (N, N))
            run1 = jnp.broadcast_to(r_t[rows, 2 * j + 1 : 2 * j + 2], (N, N))
            size = pair_of(step_t, rows, j, N)[0]
            decays = [
                jnp.exp(jnp.where(mask, r[2 * j + k : 2 * j + k + 1, rows] - col, OFF))
                for k, col in enumerate((run0, run1))
            ]
            high, low = halves(d_y[rows, at])
            mixing = jnp.concatenate([(decay * scores).astype(bf16) for decay in decays], axis=1)
            v[rows, at] = dot(mixing, stacked(high)) + dot(mixing, stacked(low))
            sized = (x[rows, at].astype(f32) * size).astype(bf16)
            both = stacked(sized)
            product = dot(both, high, NT) + dot(both, low, NT)
            total = total + product[:N] * decays[0] + product[N:] * decays[1]
        ds[b] = total.astype(bf16)
        return carry

    lax.fori_loop(0, NB, step, 0)


def backward_rest(x, bm, cm, r_t, step_t, skip, d_y, v, ds, xw, erdy, sin, gl, qd, arriving, ge, psi, own, d_x, d_b, d_c):
    def step(b, carry):
        base = pl.multiple_of(b * N, N)
        rows = pl.ds(base, N)
        b_blk, c_blk = bm[rows, :], cm[rows, :]
        for j in range(NP):
            at = lanes(j)
            run = pair_of(r_t, rows, j, N)[0]
            size = pair_of(step_t, rows, j, N)[0]
            last = pair_of(r_t, pl.ds(base + N - 1, 1), j, 1)[0]
            grad = gl[b, :, at] + qd[b, :, at] * arriving[:, at]
            passing = grad * sin[b, :, at]
            psi[b, :, at] = jnp.exp(last) * jnp.sum(passing.reshape(N // 8, 8, N), axis=0)
            high, low = halves(grad)
            ge[0, :, at] = high
            ge[1, :, at] = low
            local = v[rows, at]
            reach = dot(b_blk, high) + dot(b_blk, low)
            carried = jnp.exp(last - run) * reach
            x_val = x[rows, at].astype(f32)
            sized = x_val * size
            d_x[rows, at] = (size * (local + carried) + skip[:, at] * d_y[rows, at]).astype(bf16)
            own[rows, at] = sized.astype(bf16).astype(f32) * local
            v[rows, at] = xw[rows, at].astype(f32) * reach
            d_y[rows, at] = x_val * (local + carried)
        d_b[rows, :] = (dot(ds[b], c_blk) + dot(xw[rows, :], ge[0], NT) + dot(xw[rows, :], ge[1], NT)).astype(bf16)
        late = sin[b].astype(bf16)
        d_c[rows, :] = (dot(ds[b], b_blk, TN) + dot(erdy[0, rows, :], late, NT) + dot(erdy[1, rows, :], late, NT)).astype(bf16)
        return carry

    lax.fori_loop(0, NB, step, 0)


def steps_grad(dt, bias, alog, step, psi, row_own, row_carried, own, carried, whole, out):
    row, col = iota((N, N), 0), iota((N, N), 1)
    since = (row >= col).astype(f32)
    before = (row < col).astype(f32)
    raw = dt[...] + bias[...]
    sig = 1.0 / (1.0 + jnp.exp(-raw))
    pull = jnp.exp(alog[...])
    ones = head_rows().astype(f32)
    for b in range(NB):
        at = lanes(b)
        past = jnp.sum(dot(ones, psi[b], NT, HI), axis=1, keepdims=True)
        d_rate = dot(row_own[:, at] - own[:, at] + row_carried[:, at], since, precision=HI) + past
        d_rate = d_rate + dot(carried[:, at], before, precision=HI)
        out[:, at] = (whole[:, at] - pull * d_rate) * sig[:, at]
MESH = pl.DeviceIdType.MESH
SHARD = 128
HALF = HP // 2
D = 4096


def mod(value, size):
    return lax.rem(value + size, size)


def greet(seqs, heads):
    barrier = pltpu.get_barrier_semaphore()
    for s in seqs:
        pl.semaphore_signal(barrier, inc=1, device_id={"seq": s}, device_id_type=MESH)
    for h in heads:
        pl.semaphore_signal(barrier, inc=1, device_id={"head": h}, device_id_type=MESH)
    pl.semaphore_wait(barrier, len(seqs) + len(heads))


def greet_all(me):
    barrier = pltpu.get_barrier_semaphore()

    def step(k, carry):
        pl.semaphore_signal(barrier, inc=1, device_id={"seq": lax.rem(me + k, SEQ)}, device_id_type=MESH)
        return carry

    lax.fori_loop(1, SEQ, step, 0)
    pl.semaphore_wait(barrier, SEQ - 1)


def remote(src, dst, ssem, rsem, **device):
    return pltpu.make_async_remote_copy(
        src_ref=src, dst_ref=dst, send_sem=ssem, recv_sem=rsem, device_id=device, device_id_type=MESH
    )


SLICE = 32


def each_other(me, fn):
    def step(k, carry):
        fn(lax.rem(me + k, SEQ))
        return carry

    lax.fori_loop(1, SEQ, step, 0)


def to_copy(me, buf, land, ssem, rsem, other):
    return remote(buf.at[other], land.at[me], ssem.at[other], rsem.at[me], seq=other)


def from_copy(me, buf, land, ssem, rsem, other):
    return remote(buf.at[me], land.at[other], ssem.at[me], rsem.at[other], seq=other)


def exchange_out(me, state, decay, out1, in1, s1, r1):
    for j in range(NP):
        for i in range(N // SLICE):
            k = j * (N // SLICE) + i
            out1[k, :SLICE] = state[SLICE * i : SLICE * (i + 1), lanes(j)]
            out1[k, SLICE:] = jnp.broadcast_to(decay[:, lanes(j)], (8, N))
    each_other(me, lambda o: to_copy(me, out1, in1, s1, r1, o).start())
    in1[me] = out1[me]


def exchange_fold(me, backward, out1, in1, s1, r1, out2, in2, s2, r2):
    each_other(me, lambda o: from_copy(me, out1, in1, s1, r1, o).wait_recv())

    def step(i, total):
        at = SEQ - 1 - i if backward else i
        out2[at] = total
        return total * in1[at, SLICE : SLICE + 1] + in1[at, :SLICE]

    lax.fori_loop(0, SEQ, step, jnp.zeros((SLICE, N), f32))
    each_other(me, lambda o: to_copy(me, out2, in2, s2, r2, o).start())
    in2[me] = out2[me]


def exchange_in(me, result, out1, in1, s1, r1, out2, in2, s2, r2):
    each_other(me, lambda o: from_copy(me, out2, in2, s2, r2, o).wait_recv())
    for j in range(NP):
        for i in range(N // SLICE):
            result[SLICE * i : SLICE * (i + 1), lanes(j)] = in2[j * (N // SLICE) + i]

    def done(o):
        to_copy(me, out1, in1, s1, r1, o).wait_send()
        to_copy(me, out2, in2, s2, r2, o).wait_send()

    each_other(me, done)


EXCHANGE = [
    pltpu.VMEM((SEQ, SLICE + 8, N), f32),
    pltpu.VMEM((SEQ, SLICE + 8, N), f32),
    pltpu.SemaphoreType.DMA((SEQ,)),
    pltpu.SemaphoreType.DMA((SEQ,)),
    pltpu.VMEM((SEQ, SLICE, N), f32),
    pltpu.VMEM((SEQ, SLICE, N), f32),
    pltpu.SemaphoreType.DMA((SEQ,)),
    pltpu.SemaphoreType.DMA((SEQ,)),
]


class Torus:
    def __init__(self, half):
        self.half = half
        me = lax.axis_index("seq")
        x, y = lax.rem(me, 4), lax.rem(lax.div(me, 4), 4)
        self.z = lax.div(me, 16)
        self.p, self.q = (x, y) if half == 0 else (y, x)

    def at(self, z, p, q):
        return z * 16 + (q * 4 + p if self.half == 0 else p * 4 + q)

    def place(self, dz=0, dp=0, dq=0):
        z = 1 - self.z if dz else self.z
        return self.at(z, mod(self.p + dp, 4), mod(self.q + dq, 4))


def neighbours():
    t = Torus(0)
    return [t.place(dz=1), t.place(dp=1), t.place(dp=-1), t.place(dq=1), t.place(dq=-1)]


class Gather:
    def __init__(self, half, buf, ssem, rsem):
        self.t, self.half, self.buf, self.ssem, self.rsem, self.n = Torus(half), half, buf, ssem, rsem, 0
        self.sent = []

    def copy(self, shard, to, index):
        ref = self.buf.at[self.half, shard]
        return remote(ref, ref, self.ssem.at[self.half, index], self.rsem.at[self.half, shard], seq=to)

    def send(self, shard, to):
        copy = self.copy(shard, to, self.n)
        copy.start()
        self.sent.append(copy)
        self.n += 1

    def wait(self, shard):
        self.copy(shard, self.t.place(dz=1), 0).wait_recv()

    def spread(self, shard):
        self.send(shard, self.t.place(dq=1))
        self.send(shard, self.t.place(dq=-1))

    def own(self):
        t = self.t
        mine = t.place()
        self.send(mine, t.place(dz=1))
        self.send(mine, t.place(dp=1))
        self.send(mine, t.place(dp=-1))
        self.spread(mine)

    def across(self):
        t = self.t
        other = t.place(dz=1)
        self.wait(other)
        self.send(other, t.place(dp=1))
        self.send(other, t.place(dp=-1))
        self.spread(other)

    def near(self):
        t = self.t
        for z in (0, 1):
            for dp in (-1, 1):
                shard = t.at(z, mod(t.p + dp, 4), t.q)
                self.wait(shard)
                if (z, dp) in ((0, -1), (1, 1)):
                    self.send(shard, t.place(dp=-dp))
                self.spread(shard)

    def far(self):
        t = self.t
        for z in (0, 1):
            shard = t.at(z, mod(t.p + 2, 4), t.q)
            self.wait(shard)
            self.spread(shard)

    def pass_on(self):
        t = self.t
        for k in range(4):
            p = mod(t.p + (0, 1, 3, 2)[k], 4)
            for z, dq in ((0, -1), (1, 1)):
                shard = t.at(z, p, mod(t.q + dq, 4))
                self.wait(shard)
                self.send(shard, t.place(dq=-dq))

    def rest(self):
        t = self.t
        for p in range(4):
            for z, dq in ((1, -1), (0, 1), (0, 2), (1, 2)):
                self.wait(t.at(z, p, mod(t.q + dq, 4)))

    def close(self):
        for copy in self.sent:
            copy.wait_send()


class Heads:
    PARTS = 2

    def __init__(self, buf, ssem, rsem):
        self.h = lax.axis_index("head")
        self.core = self.h + 1 - 2 * lax.rem(self.h, 2)
        self.chip = lax.rem(self.h + 2, 4)
        self.buf, self.ssem, self.rsem, self.sent = buf, ssem, rsem, []

    def copy(self, block, part, to, index):
        ref = self.buf.at[block, pl.ds(part * (T // self.PARTS), T // self.PARTS)]
        return remote(ref, ref, self.ssem.at[index], self.rsem.at[block, part], head=to)

    def send(self, block, part, to):
        copy = self.copy(block, part, to, len(self.sent))
        copy.start()
        self.sent.append(copy)

    def own(self):
        for part in range(self.PARTS):
            self.send(self.h, part, self.chip)
        for part in range(self.PARTS):
            self.send(self.h, part, self.core)

    def across(self):
        for part in range(self.PARTS):
            self.copy(self.chip, part, self.chip, 0).wait_recv()
            self.send(self.chip, part, self.core)

    def rest(self):
        for part in range(self.PARTS):
            self.copy(self.core, part, self.core, 0).wait_recv()
            self.copy(lax.rem(self.core + 2, 4), part, self.core, 0).wait_recv()

    def close(self):
        for copy in self.sent:
            copy.wait_send()


FARP, FARM, NEARP, NEARM, PFARP, PFARM, PNEARP, PNEARM, ACROSS = 0, 4, 8, 16, 24, 25, 26, 28, 30
SLOTS = 31


class Scatter:
    def __init__(self, half, part, out, inn, ssem, rsem, acc, result):
        self.t, self.half, self.part, self.out, self.inn = Torus(half), half, part, out, inn
        self.ssem, self.rsem, self.acc, self.result = ssem, rsem, acc, result

    def copy(self, slot, to):
        h = self.half
        return remote(self.out.at[h, slot], self.inn.at[h, slot], self.ssem.at[h, slot], self.rsem.at[h, slot], seq=to)

    def send(self, slot, value, to):
        self.out[self.half, slot] = value.astype(bf16)
        self.copy(slot, to).start()

    def got(self, slot):
        self.copy(slot, self.t.place(dz=1)).wait_recv()
        return self.inn[self.half, slot].astype(f32)

    def loop(self, fn):
        def step(p, carry):
            fn(p)
            return carry

        lax.fori_loop(0, 4, step, 0)

    def q_far(self):
        t = self.t
        far = mod(t.q + 2, 4)

        def fn(p):
            self.send(FARP + p, self.part(self.half, t.at(0, p, far)), t.place(dq=1))
            self.send(FARM + p, self.part(self.half, t.at(1, p, far)), t.place(dq=-1))

        self.loop(fn)

    def q_near(self):
        t = self.t
        up, down = mod(t.q + 1, 4), mod(t.q - 1, 4)

        def fn(p):
            self.send(NEARP + 4 + p, self.part(self.half, t.at(1, p, up)), t.place(dq=1))
            self.send(NEARM + p, self.part(self.half, t.at(0, p, down)), t.place(dq=-1))

        self.loop(fn)

    def q_pass(self):
        t = self.t
        up, down = mod(t.q + 1, 4), mod(t.q - 1, 4)

        def fn(p):
            self.send(NEARP + p, self.part(self.half, t.at(0, p, up)) + self.got(FARP + p), t.place(dq=1))
            self.send(NEARM + 4 + p, self.part(self.half, t.at(1, p, down)) + self.got(FARM + p), t.place(dq=-1))

        self.loop(fn)

    def q_own(self):
        t = self.t

        def fn(p):
            for z in (0, 1):
                self.acc[self.half, z, p] = self.part(self.half, t.at(z, p, t.q))

        self.loop(fn)

    def total(self, z, p):
        return self.acc[self.half, z, p] + self.got(NEARP + 4 * z + p) + self.got(NEARM + 4 * z + p)

    def p_far(self):
        t = self.t
        far = mod(t.p + 2, 4)
        self.send(PFARP, self.total(0, far), t.place(dp=1))
        self.send(PFARM, self.total(1, far), t.place(dp=-1))

    def p_near(self):
        t = self.t
        up, down = mod(t.p + 1, 4), mod(t.p - 1, 4)
        self.send(PNEARP + 1, self.total(1, up), t.place(dp=1))
        self.send(PNEARM, self.total(0, down), t.place(dp=-1))
        self.send(PNEARP, self.total(0, up) + self.got(PFARP), t.place(dp=1))
        self.send(PNEARM + 1, self.total(1, down) + self.got(PFARM), t.place(dp=-1))

    def p_own(self):
        t = self.t
        for z in (0, 1):
            self.acc[self.half, z, t.p] = self.total(z, t.p)

    def p_sum(self, z):
        return self.acc[self.half, z, self.t.p] + self.got_at(PNEARP, z) + self.got_at(PNEARM, z)

    def got_at(self, base, z):
        return self.got(base + z)

    def z_out(self):
        t = self.t
        self.send(ACROSS, self.p_sum(1 - t.z), t.place(dz=1))

    def z_in(self):
        t = self.t
        self.result[:, HALF * self.half : HALF * (self.half + 1)] = self.p_sum(t.z) + self.got(ACROSS)

    def close(self):
        def step(slot, carry):
            self.copy(slot, self.t.place(dz=1)).wait_send()
            return carry

        lax.fori_loop(0, SLOTS, step, 0)


V = pltpu.VMEM
DMA = pltpu.SemaphoreType.DMA


def call(fn, outs, scratch, *args, cid=None):
    return pl.pallas_call(
        fn,
        out_shape=[jax.ShapeDtypeStruct(s, d) for s, d in outs],
        in_specs=[pl.BlockSpec(memory_space=pltpu.VMEM)] * len(args),
        out_specs=[pl.BlockSpec(memory_space=pltpu.VMEM)] * len(outs),
        scratch_shapes=scratch,
        compiler_params=pltpu.CompilerParams(vmem_limit_bytes=60 << 20, collective_id=cid, has_side_effects=cid is not None),
    )(*args)


def k1(x, bm, cm, dt, bias, alog, keep_t, within, er, xw, sl, pd, step, r, step_t, r_t, st):
    prepare(dt, bias, alog, step, r, step_t, r_t)
    forward_local(x, bm, cm, r, r_t, step_t, keep_t, within, er, xw, sl, pd, st)


def k2(x, cm, sl, pd, entering, er, skip, within, z, gain, y, sin, normed):
    enter(x, cm, sl, pd, entering, er, skip, within, y, sin)
    norm(y, z, gain, normed)


def k3(y, within, x, z, gain, skip, d_normed, cm, r_t, keep_t, er, d_z, d_y, row_own, row_carried, erdy, gl, qd, gt, work, carried):
    unnorm(y, within, x, z, gain, skip, d_normed, d_z, d_y, work, carried)
    gather_heads(work, row_own)
    gather_heads(carried, row_carried)
    state_grad(cm, r_t, keep_t, er, d_y, erdy, gl, qd, gt)


def k4(x, bm, cm, r, r_t, step_t, skip, d_y0, xw, erdy, sin, gl, qd, arriving,
       dt, bias, alog, step, row_own, row_carried, d_x, d_b, d_c, out, d_y, v, ds, ge, psi, own, s1, s2, s3):
    d_y[...] = d_y0[...]
    backward_within(x, bm, cm, r, r_t, step_t, d_y, v, ds)
    backward_rest(x, bm, cm, r_t, step_t, skip, d_y, v, ds, xw, erdy, sin, gl, qd, arriving, ge, psi, own, d_x, d_b, d_c)
    gather_heads(own, s1)
    gather_heads(v, s2)
    gather_heads(d_y, s3)
    steps_grad(dt, bias, alog, step, psi, row_own, row_carried, s1, s2, s3, out)


def kx(backward, state, decay, result, *bufs):
    me = lax.axis_index("seq")
    greet_all(me)
    exchange_out(me, state, decay, *bufs[:4])
    exchange_fold(me, backward, *bufs)
    exchange_in(me, result, *bufs)


def multiply(cots, ws, out):
    def step(i, carry):
        half, tile = lax.div(i, 2), lax.rem(i, 2)
        at = pl.ds(pl.multiple_of(tile * 256, 256), 256)
        total = None
        for k in range(4):
            rows = ws[half, 8 * k : 8 * k + 8, :, at].reshape(1024, 256)
            term = dot(cots[k], rows)
            total = term if total is None else total + term
        out[:, pl.ds(pl.multiple_of(i * 256, 256), 256)] = total
        return carry

    lax.fori_loop(0, 4, step, 0)


def kg(w, cot, d_normed, cots, wbuf, cbuf, ws, wr, cs, cr):
    heads = Heads(cbuf, cs, cr)
    gathers = [Gather(h, wbuf, ws, wr) for h in (0, 1)]
    me = lax.axis_index("seq")
    wbuf[0, me] = w[:, :HALF]
    wbuf[1, me] = w[:, HALF:]
    cbuf[heads.h] = cot[...]
    greet(neighbours(), [heads.core, heads.chip])
    for name in ("own", "across", "near", "far", "pass_on", "rest"):
        for g in gathers:
            getattr(g, name)()
        if name in ("own", "across", "rest"):
            getattr(heads, name)()
    multiply(cbuf, wbuf, d_normed)
    cots[...] = cbuf[...]
    for g in gathers:
        g.close()
    heads.close()


def ks(cots, normed, result, out, inn, ss, rs, acc):
    def part(half, shard):
        block, at = lax.div(shard, 8), lax.rem(shard, 8)
        cols = pl.ds(pl.multiple_of(at * SHARD, SHARD), SHARD)
        return dot(cots[block, :, cols], normed[:, HALF * half : HALF * (half + 1)], TN)

    greet(neighbours(), [])
    scatters = [Scatter(h, part, out, inn, ss, rs, acc, result) for h in (0, 1)]
    for name in ("q_far", "q_near", "q_pass", "q_own", "p_far", "p_near", "p_own", "z_out", "z_in", "close"):
        for s in scatters:
            getattr(s, name)()


def body(x, z, bm, cm, dt, bias, alog, skip, gain, resets, w, cot):
    keep = 1.0 - resets.astype(f32)
    keep_t = keep.T[:, None, :]
    skip = jnp.repeat(skip, 64)[None]
    gain = gain[None]
    bias, alog = bias[:, None], alog[:, None]
    F, B = f32, bf16
    within, er, xw, sl, pd, step, r, step_t, r_t = call(
        k1, [((T, HP), F), ((T, HP), F), ((T, HP), B), ((NB + 1, N, HP), F), ((NB + 1, 1, HP), F), ((H, T), F), ((H, T), F), ((T, H), F), ((T, H), F)],
        [V((N, HP), F)], x, bm, cm, dt, bias, alog, keep_t)
    entering = call(functools.partial(kx, False), [((N, HP), F)], EXCHANGE, sl[NB], pd[NB], cid=0)[0]
    y, sin, normed = call(k2, [((T, HP), F), ((NB, N, HP), F), ((T, HP), B)], [], x, cm, sl, pd, entering, er, skip, within, z, gain)
    d_normed, cots = call(
        kg, [((T, HP), F), ((4, T, HP), B)],
        [V((2, SEQ, SHARD, HALF), B), V((4, T, HP), B), DMA((2, 31)), DMA((2, SEQ)), DMA((6,)), DMA((4, 2))], w, cot, cid=2)
    d_z, d_y, row_own, row_carried, erdy, gl, qd, gt = call(
        k3, [((T, HP), B), ((T, HP), F), ((H, T), F), ((H, T), F), ((2, T, HP), B), ((NB, N, HP), F), ((NB + 1, 1, HP), F), ((N, HP), F)],
        [V((T, HP), F), V((T, HP), F)], y, within, x, z, gain, skip, d_normed, cm, r_t, keep_t, er)
    arriving = call(functools.partial(kx, True), [((N, HP), F)], EXCHANGE, gt, pd[NB], cid=1)[0]
    d_x, d_b, d_c, out = call(
        k4, [((T, HP), B), ((T, N), B), ((T, N), B), ((H, T), F)],
        [V((T, HP), F), V((T, HP), F), V((NB, N, N), B), V((2, N, HP), B), V((NB, 8, HP), F), V((T, HP), F), V((H, T), F), V((H, T), F), V((H, T), F)],
        x, bm, cm, r, r_t, step_t, skip, d_y, xw, erdy, sin, gl, qd, arriving, dt, bias, alog, step, row_own, row_carried)
    d_w = call(
        ks, [((SHARD, HP), F)],
        [V((2, SLOTS, SHARD, HALF), B), V((2, SLOTS, SHARD, HALF), B), DMA((2, SLOTS)), DMA((2, SLOTS)), V((2, 2, 4, SHARD, HALF), F)],
        cots, normed, cid=3)[0]
    return d_x, d_z, d_b, d_c, out, d_w


def solution(mesh):
    s, h = P("seq", "head"), P("head")
    return jax.shard_map(
        body, mesh=mesh,
        in_specs=(s, s, s, s, P("head", "seq"), h, h, h, h, P("head", "seq"), s, s),
        out_specs=(s, s, s, s, P("head", "seq"), s), check_vma=False)
```

```python
import jax
import jax.numpy as jnp
from jax import lax
from jax.experimental import pallas as pl
from jax.experimental.pallas import tpu as pltpu
from jax.sharding import PartitionSpec as P

T = 512
N = 128
HP = 1024
H = 16
NB = T // N
NP = HP // N
SEQ = 32

f32 = jnp.float32
bf16 = jnp.bfloat16
HI = lax.Precision.HIGHEST
NN = (((1,), (0,)), ((), ()))
NT = (((1,), (1,)), ((), ()))
TN = (((0,), (0,)), ((), ()))
OFF = -1e30


def dot(a, b, dims=NN, precision=None):
    return lax.dot_general(a, b, dims, precision=precision, preferred_element_type=f32)


def iota(shape, axis):
    return lax.broadcasted_iota(jnp.int32, shape, axis)


def pair_of(ref, rows, j, count):
    first = jnp.broadcast_to(ref[rows, 2 * j : 2 * j + 1], (count, N))
    second = jnp.broadcast_to(ref[rows, 2 * j + 1 : 2 * j + 2], (count, N))
    return jnp.where(iota((count, N), 1) < 64, first, second), first, second


def head_rows():
    row, col = iota((H, HP), 0), iota((H, HP), 1)
    return ((col >= 64 * row) & (col < 64 * row + 64)).astype(bf16)


def halves(value):
    high = value.astype(bf16)
    return high, (value - high.astype(f32)).astype(bf16)


def head_sums(value):
    high, low = halves(value)
    ones = head_rows()
    return dot(ones, high, NT) + dot(ones, low, NT)


def stacked(value):
    low = iota(value.shape, 1) < 64
    zero = jnp.zeros_like(value)
    return jnp.concatenate([jnp.where(low, value, zero), jnp.where(low, zero, value)], axis=0)


def lanes(j):
    return slice(N * j, N * j + N)


def column(ref):
    eye = iota((H, H), 0) == iota((H, H), 1)
    return jnp.sum(jnp.where(eye, jnp.broadcast_to(ref[...], (H, H)), 0.0), axis=1, keepdims=True)


def prepare(dt, bias, alog, resets, skip, step, r, step_t, r_t, keep_t, skips):
    raw = dt[...] + column(bias)
    step[...] = jnp.maximum(raw, 0.0) + jnp.log1p(jnp.exp(-jnp.abs(raw)))
    rate = -step[...] * jnp.exp(column(alog))
    keep = 1.0 - resets[...].astype(f32)
    square = iota((H, H), 0) == iota((H, H), 1)
    for b in range(NB):
        spread = jnp.where(square, jnp.broadcast_to(keep[:, b : b + 1], (H, H)), 0.0)
        keep_t[b] = jnp.sum(spread, axis=0, keepdims=True)
    for j in range(NP):
        skips[:, lanes(j)] = pair_of(skip, slice(0, 1), j, 1)[0]
    row, col = iota((N, N), 0), iota((N, N), 1)
    upper = (row <= col).astype(f32)
    eye = (row == col).astype(f32)
    for b in range(NB):
        at = lanes(b)
        r[:, at] = dot(rate[:, at], upper, precision=HI)
        r_t[at, :] = dot(eye, r[:, at], NT, HI)
        step_t[at, :] = dot(eye, step[:, at], NT, HI)


def forward_block(b, x, bm, cm, r, r_t, step_t, keep_t, within, er, xw, sl, pd, st):
    base = b * N
    rows = pl.ds(base, N)
    mask = iota((N, N), 0) >= iota((N, N), 1)
    b_blk, c_blk = bm[rows, :], cm[rows, :]
    b_flip = b_blk.astype(f32).T.astype(bf16)
    scores = dot(c_blk, b_blk, NT)
    for j in range(NP):
        at = lanes(j)
        run, run0, run1 = pair_of(r_t, rows, j, N)
        size = pair_of(step_t, rows, j, N)[0]
        last = pair_of(r_t, pl.ds(base + N - 1, 1), j, 1)[0]
        keep = pair_of(keep_t.at[b], slice(0, 1), j, 1)[0]
        mixing = [
            (jnp.exp(jnp.where(mask, col - r[2 * j + k : 2 * j + k + 1, rows], OFF)) * scores).astype(bf16)
            for k, col in enumerate((run0, run1))
        ]
        x_val = x[rows, at].astype(f32)
        sized = x_val * size
        within[rows, at] = dot(jnp.concatenate(mixing, axis=1), stacked(sized.astype(bf16)))
        er[rows, at] = jnp.exp(run)
        weighted = (sized * jnp.exp(last - run)).astype(bf16)
        xw[rows, at] = weighted
        state = st[:, at] * keep
        sl[b, :, at] = state
        span = pd[b, :, at] * keep
        pd[b, :, at] = span
        decay = jnp.exp(last)
        pd[b + 1, :, at] = span * decay
        st[:, at] = state * decay + dot(b_flip, weighted)


def forward_start(pd, st):
    st[...] = jnp.zeros_like(st)
    pd[0] = jnp.ones((1, HP), f32)


def enter(x, cm, sl, pd, entering, er, skip, within, y):
    def step(b, carry):
        rows = pl.ds(pl.multiple_of(b * N, N), N)
        c_blk = cm[rows, :]
        for j in range(NP):
            at = lanes(j)
            state = sl[b, :, at] + pd[b, :, at] * entering[:, at]
            sl[b, :, at] = state
            high, low = halves(state)
            y[rows, at] = within[rows, at] + (dot(c_blk, high) + dot(c_blk, low)) * er[rows, at] + skip[:, at] * x[rows, at].astype(f32)
        return carry

    lax.fori_loop(0, NB, step, 0)


CH = 32


def norm(y, z, gain, normed):
    def step(i, carry):
        rows = pl.ds(pl.multiple_of(i * CH, CH), CH)
        z_val = z[rows, :].astype(f32)
        gated = y[rows, :] * (z_val / (1.0 + jnp.exp(-z_val)))
        factor = lax.rsqrt(jnp.mean(gated * gated, axis=1, keepdims=True) + 1e-05)
        normed[rows, :] = (gated * factor * gain[...]).astype(bf16)
        return carry

    lax.fori_loop(0, T // CH, step, 0)


def unnorm(y, within, x, z, gain, skip, d_normed, d_z, d_y):
    def step(i, carry):
        rows = pl.ds(pl.multiple_of(i * CH, CH), CH)
        z_val = z[rows, :].astype(f32)
        y_val = y[rows, :]
        sig = 1.0 / (1.0 + jnp.exp(-z_val))
        silu = z_val * sig
        gated = y_val * silu
        factor = lax.rsqrt(jnp.mean(gated * gated, axis=1, keepdims=True) + 1e-05)
        scaled = d_normed[rows, :] * gain[...]
        along = jnp.mean(scaled * gated, axis=1, keepdims=True)
        d_gated = factor * scaled - gated * (factor * factor * factor * along)
        d_z[rows, :] = (d_gated * y_val * (sig * (1.0 + z_val * (1.0 - sig)))).astype(bf16)
        d_mixed = d_gated * silu
        d_y[rows, :] = d_mixed
        own = within[rows, :]
        y[rows, :] = d_mixed * own
        d_normed[rows, :] = d_mixed * (y_val - skip[...] * x[rows, :].astype(f32) - own)
        return carry

    lax.fori_loop(0, T // CH, step, 0)


def gather_heads(work, sums):
    def step(b, carry):
        rows = pl.ds(pl.multiple_of(b * N, N), N)
        sums[:, rows] = head_sums(work[rows, :])
        return carry

    lax.fori_loop(0, NB, step, 0)


def state_grad(cm, r_t, keep_t, er, d_y, gl, qd, gt):
    gt[...] = jnp.zeros_like(gt)
    qd[NB - 1] = jnp.ones((1, HP), f32)

    def step(i, carry):
        b = NB - 1 - i
        base = pl.multiple_of(b * N, N)
        rows = pl.ds(base, N)
        c_flip = cm[rows, :].astype(f32).T.astype(bf16)
        for j in range(NP):
            at = lanes(j)
            last = pair_of(r_t, pl.ds(base + N - 1, 1), j, 1)[0]
            keep = pair_of(keep_t.at[b], slice(0, 1), j, 1)[0]
            high, low = halves(er[rows, at] * d_y[rows, at])
            grad = gt[:, at]
            gl[b, :, at] = grad
            decay = jnp.exp(last)
            gt[:, at] = keep * (decay * grad + dot(c_flip, high) + dot(c_flip, low))
            value = qd[b, :, at]

            @pl.when(b > 0)
            def _():
                qd[b - 1, :, at] = keep * decay * value

        return carry

    lax.fori_loop(0, NB, step, 0)


def backward_within(x, bm, cm, r, r_t, step_t, d_y, v, ds):
    def step(b, carry):
        rows = pl.ds(pl.multiple_of(b * N, N), N)
        mask = iota((N, N), 0) <= iota((N, N), 1)
        scores = dot(bm[rows, :], cm[rows, :], NT)
        total = jnp.zeros((N, N), f32)
        for j in range(NP):
            at = lanes(j)
            run0 = jnp.broadcast_to(r_t[rows, 2 * j : 2 * j + 1], (N, N))
            run1 = jnp.broadcast_to(r_t[rows, 2 * j + 1 : 2 * j + 2], (N, N))
            size = pair_of(step_t, rows, j, N)[0]
            decays = [
                jnp.exp(jnp.where(mask, r[2 * j + k : 2 * j + k + 1, rows] - col, OFF))
                for k, col in enumerate((run0, run1))
            ]
            high, low = halves(d_y[rows, at])
            mixing = jnp.concatenate([(decay * scores).astype(bf16) for decay in decays], axis=1)
            v[rows, at] = dot(mixing, stacked(high)) + dot(mixing, stacked(low))
            sized = (x[rows, at].astype(f32) * size).astype(bf16)
            both = stacked(sized)
            product = dot(both, high, NT) + dot(both, low, NT)
            total = total + product[:N] * decays[0] + product[N:] * decays[1]
        ds[b] = total.astype(bf16)
        return carry

    lax.fori_loop(0, NB, step, 0)


def backward_rest(x, bm, cm, r_t, step_t, skip, d_y, v, ds, xw, er, sl, gl, qd, arriving, ge, gy, psi, own, d_x, d_b, d_c):
    def step(b, carry):
        base = pl.multiple_of(b * N, N)
        rows = pl.ds(base, N)
        b_blk, c_blk = bm[rows, :], cm[rows, :]
        for j in range(NP):
            at = lanes(j)
            run = pair_of(r_t, rows, j, N)[0]
            size = pair_of(step_t, rows, j, N)[0]
            last = pair_of(r_t, pl.ds(base + N - 1, 1), j, 1)[0]
            grad = gl[b, :, at] + qd[b, :, at] * arriving[:, at]
            passing = grad * sl[b, :, at]
            psi[b, :, at] = jnp.exp(last) * jnp.sum(passing.reshape(N // 8, 8, N), axis=0)
            high, low = halves(grad)
            ge[0, :, at] = high
            ge[1, :, at] = low
            local = v[rows, at]
            gy[0, :, at], gy[1, :, at] = halves(er[rows, at] * d_y[rows, at])
            reach = dot(b_blk, high) + dot(b_blk, low)
            carried = jnp.exp(last - run) * reach
            x_val = x[rows, at].astype(f32)
            sized = x_val * size
            d_x[rows, at] = (size * (local + carried) + skip[:, at] * d_y[rows, at]).astype(bf16)
            own[rows, at] = sized.astype(bf16).astype(f32) * local
            v[rows, at] = xw[rows, at].astype(f32) * reach
            d_y[rows, at] = x_val * (local + carried)
        d_b[rows, :] = (dot(ds[b], c_blk) + dot(xw[rows, :], ge[0], NT) + dot(xw[rows, :], ge[1], NT)).astype(bf16)
        late = sl[b].astype(bf16)
        d_c[rows, :] = (dot(ds[b], b_blk, TN) + dot(gy[0], late, NT) + dot(gy[1], late, NT)).astype(bf16)
        return carry

    lax.fori_loop(0, NB, step, 0)


def steps_grad(dt, bias, alog, step, psi, row_own, row_carried, own, carried, whole, out):
    row, col = iota((N, N), 0), iota((N, N), 1)
    since = (row >= col).astype(f32)
    before = (row < col).astype(f32)
    raw = dt[...] + column(bias)
    sig = 1.0 / (1.0 + jnp.exp(-raw))
    pull = jnp.exp(column(alog))
    ones = head_rows().astype(f32)
    for b in range(NB):
        at = lanes(b)
        past = jnp.sum(dot(ones, psi[b], NT, HI), axis=1, keepdims=True)
        d_rate = dot(row_own[:, at] - own[:, at] + row_carried[:, at], since, precision=HI) + past
        d_rate = d_rate + dot(carried[:, at], before, precision=HI)
        out[:, at] = (whole[:, at] - pull * d_rate) * sig[:, at]


MESH = pl.DeviceIdType.MESH
SHARD = 128
HALF = HP // 2
D = 4096


def mod(value, size):
    return lax.rem(value + size, size)


def greet(me, heads):
    barrier = pltpu.get_barrier_semaphore()

    def step(k, carry):
        pl.semaphore_signal(barrier, inc=1, device_id={"seq": lax.rem(me + k, SEQ)}, device_id_type=MESH)
        return carry

    lax.fori_loop(1, SEQ, step, 0)
    for h in heads:
        pl.semaphore_signal(barrier, inc=1, device_id={"head": h}, device_id_type=MESH)
    pl.semaphore_wait(barrier, SEQ - 1 + len(heads))


def remote(src, dst, ssem, rsem, **device):
    return pltpu.make_async_remote_copy(
        src_ref=src, dst_ref=dst, send_sem=ssem, recv_sem=rsem, device_id=device, device_id_type=MESH
    )


SLICE = 32


def each_other(me, fn):
    def step(k, carry):
        fn(lax.rem(me + k, SEQ))
        return carry

    lax.fori_loop(1, SEQ, step, 0)


def to_copy(me, buf, land, ssem, rsem, other):
    return remote(buf.at[other], land.at[me], ssem.at[other], rsem.at[me], seq=other)


def from_copy(me, buf, land, ssem, rsem, other):
    return remote(buf.at[me], land.at[other], ssem.at[me], rsem.at[other], seq=other)


def exchange_out(me, state, decay, out1, in1, s1, r1):
    for j in range(NP):
        for i in range(N // SLICE):
            k = j * (N // SLICE) + i
            out1[k, :SLICE] = state[SLICE * i : SLICE * (i + 1), lanes(j)]
            out1[k, SLICE:] = jnp.broadcast_to(decay[:, lanes(j)], (8, N))
    each_other(me, lambda o: to_copy(me, out1, in1, s1, r1, o).start())
    in1[me] = out1[me]


def exchange_fold(me, backward, out1, in1, s1, r1, out2, in2, s2, r2):
    each_other(me, lambda o: from_copy(me, out1, in1, s1, r1, o).wait_recv())

    def step(i, total):
        at = SEQ - 1 - i if backward else i
        out2[at] = total
        return total * in1[at, SLICE : SLICE + 1] + in1[at, :SLICE]

    lax.fori_loop(0, SEQ, step, jnp.zeros((SLICE, N), f32))
    each_other(me, lambda o: to_copy(me, out2, in2, s2, r2, o).start())
    in2[me] = out2[me]


def exchange_in(me, result, out1, in1, s1, r1, out2, in2, s2, r2):
    each_other(me, lambda o: from_copy(me, out2, in2, s2, r2, o).wait_recv())
    for j in range(NP):
        for i in range(N // SLICE):
            result[SLICE * i : SLICE * (i + 1), lanes(j)] = in2[j * (N // SLICE) + i]

    def done(o):
        to_copy(me, out1, in1, s1, r1, o).wait_send()
        to_copy(me, out2, in2, s2, r2, o).wait_send()

    each_other(me, done)


EXCHANGE = [
    pltpu.VMEM((SEQ, SLICE + 8, N), f32),
    pltpu.VMEM((SEQ, SLICE + 8, N), f32),
    pltpu.SemaphoreType.DMA((SEQ,)),
    pltpu.SemaphoreType.DMA((SEQ,)),
    pltpu.VMEM((SEQ, SLICE, N), f32),
    pltpu.VMEM((SEQ, SLICE, N), f32),
    pltpu.SemaphoreType.DMA((SEQ,)),
    pltpu.SemaphoreType.DMA((SEQ,)),
]


class Torus:
    def __init__(self, half):
        self.half = half
        me = lax.axis_index("seq")
        x, y = lax.rem(me, 4), lax.rem(lax.div(me, 4), 4)
        self.z = lax.div(me, 16)
        self.p, self.q = (x, y) if half == 0 else (y, x)

    def at(self, z, p, q):
        return z * 16 + (q * 4 + p if self.half == 0 else p * 4 + q)

    def place(self, dz=0, dp=0, dq=0):
        z = 1 - self.z if dz else self.z
        return self.at(z, mod(self.p + dp, 4), mod(self.q + dq, 4))


class Gather:
    def __init__(self, half, buf, ssem, rsem):
        self.t, self.half, self.buf, self.ssem, self.rsem, self.n = Torus(half), half, buf, ssem, rsem, 0
        self.sent = []

    def copy(self, shard, to, index):
        ref = self.buf.at[self.half, shard]
        return remote(ref, ref, self.ssem.at[self.half, index], self.rsem.at[self.half, shard], seq=to)

    def send(self, shard, to):
        copy = self.copy(shard, to, self.n)
        copy.start()
        self.sent.append(copy)
        self.n += 1

    def wait(self, shard):
        self.copy(shard, self.t.place(dz=1), 0).wait_recv()

    def spread(self, shard):
        self.send(shard, self.t.place(dq=1))
        self.send(shard, self.t.place(dq=-1))

    def own(self):
        t = self.t
        mine = t.place()
        self.send(mine, t.place(dz=1))
        self.send(mine, t.place(dp=1))
        self.send(mine, t.place(dp=-1))
        self.spread(mine)

    def across(self):
        t = self.t
        other = t.place(dz=1)
        self.wait(other)
        self.send(other, t.place(dp=1))
        self.send(other, t.place(dp=-1))
        self.spread(other)

    def near(self):
        t = self.t
        for z in (0, 1):
            for dp in (-1, 1):
                shard = t.at(z, mod(t.p + dp, 4), t.q)
                self.wait(shard)
                if (z, dp) in ((0, -1), (1, 1)):
                    self.send(shard, t.place(dp=-dp))
                self.spread(shard)

    def far(self):
        t = self.t
        for z in (0, 1):
            shard = t.at(z, mod(t.p + 2, 4), t.q)
            self.wait(shard)
            self.spread(shard)

    def pass_on(self, ks):
        t = self.t
        for k in ks:
            p = mod(t.p + (0, 1, 3, 2)[k], 4)
            for z, dq in ((0, -1), (1, 1)):
                shard = t.at(z, p, mod(t.q + dq, 4))
                self.wait(shard)
                self.send(shard, t.place(dq=-dq))

    def rest(self):
        t = self.t
        for p in range(4):
            for z, dq in ((1, -1), (0, 1), (0, 2), (1, 2)):
                self.wait(t.at(z, p, mod(t.q + dq, 4)))

    def close(self):
        for copy in self.sent:
            copy.wait_send()


class Heads:
    PARTS = 2

    def __init__(self, buf, ssem, rsem):
        self.h = lax.axis_index("head")
        self.core = self.h + 1 - 2 * lax.rem(self.h, 2)
        self.chip = lax.rem(self.h + 2, 4)
        self.buf, self.ssem, self.rsem, self.sent = buf, ssem, rsem, []

    def copy(self, block, part, to, index):
        ref = self.buf.at[block, pl.ds(part * (T // self.PARTS), T // self.PARTS)]
        return remote(ref, ref, self.ssem.at[index], self.rsem.at[block, part], head=to)

    def send(self, block, part, to):
        copy = self.copy(block, part, to, len(self.sent))
        copy.start()
        self.sent.append(copy)

    def own(self):
        for part in range(self.PARTS):
            self.send(self.h, part, self.chip)
        for part in range(self.PARTS):
            self.send(self.h, part, self.core)

    def across(self):
        for part in range(self.PARTS):
            self.copy(self.chip, part, self.chip, 0).wait_recv()
            self.send(self.chip, part, self.core)

    def rest(self):
        for part in range(self.PARTS):
            self.copy(self.core, part, self.core, 0).wait_recv()
            self.copy(lax.rem(self.core + 2, 4), part, self.core, 0).wait_recv()

    def close(self):
        for copy in self.sent:
            copy.wait_send()


FARP, FARM, NEARP, NEARM, PFARP, PFARM, PNEARP, PNEARM, ACROSS = 0, 4, 8, 16, 24, 25, 26, 28, 30
SLOTS = 31


class Scatter:
    def __init__(self, half, part, out, inn, ssem, rsem, acc, result):
        self.t, self.half, self.part, self.out, self.inn = Torus(half), half, part, out, inn
        self.ssem, self.rsem, self.acc, self.result = ssem, rsem, acc, result

    def copy(self, slot, to):
        h = self.half
        return remote(self.out.at[h, slot], self.inn.at[h, slot], self.ssem.at[h, slot], self.rsem.at[h, slot], seq=to)

    def send(self, slot, value, to):
        self.out[self.half, slot] = value.astype(bf16)
        self.copy(slot, to).start()

    def got(self, slot):
        self.copy(slot, self.t.place(dz=1)).wait_recv()
        return self.inn[self.half, slot].astype(f32)

    def loop(self, fn):
        def step(p, carry):
            fn(p)
            return carry

        lax.fori_loop(0, 4, step, 0)

    def q_far(self):
        t = self.t
        far = mod(t.q + 2, 4)

        def fn(p):
            self.send(FARP + p, self.part(self.half, t.at(0, p, far)), t.place(dq=1))
            self.send(FARM + p, self.part(self.half, t.at(1, p, far)), t.place(dq=-1))

        self.loop(fn)

    def q_near(self):
        t = self.t
        up, down = mod(t.q + 1, 4), mod(t.q - 1, 4)

        def fn(p):
            self.send(NEARP + 4 + p, self.part(self.half, t.at(1, p, up)), t.place(dq=1))
            self.send(NEARM + p, self.part(self.half, t.at(0, p, down)), t.place(dq=-1))

        self.loop(fn)

    def q_pass(self):
        t = self.t
        up, down = mod(t.q + 1, 4), mod(t.q - 1, 4)

        def fn(p):
            self.send(NEARP + p, self.part(self.half, t.at(0, p, up)) + self.got(FARP + p), t.place(dq=1))
            self.send(NEARM + 4 + p, self.part(self.half, t.at(1, p, down)) + self.got(FARM + p), t.place(dq=-1))

        self.loop(fn)

    def q_own(self):
        t = self.t

        def fn(p):
            for z in (0, 1):
                self.acc[self.half, z, p] = self.part(self.half, t.at(z, p, t.q))

        self.loop(fn)

    def total(self, z, p):
        return self.acc[self.half, z, p] + self.got(NEARP + 4 * z + p) + self.got(NEARM + 4 * z + p)

    def p_far(self):
        t = self.t
        far = mod(t.p + 2, 4)
        self.send(PFARP, self.total(0, far), t.place(dp=1))
        self.send(PFARM, self.total(1, far), t.place(dp=-1))

    def p_near(self):
        t = self.t
        up, down = mod(t.p + 1, 4), mod(t.p - 1, 4)
        self.send(PNEARP + 1, self.total(1, up), t.place(dp=1))
        self.send(PNEARM, self.total(0, down), t.place(dp=-1))
        self.send(PNEARP, self.total(0, up) + self.got(PFARP), t.place(dp=1))
        self.send(PNEARM + 1, self.total(1, down) + self.got(PFARM), t.place(dp=-1))

    def p_own(self):
        t = self.t
        for z in (0, 1):
            self.acc[self.half, z, t.p] = self.total(z, t.p)

    def p_sum(self, z):
        return self.acc[self.half, z, self.t.p] + self.got_at(PNEARP, z) + self.got_at(PNEARM, z)

    def got_at(self, base, z):
        return self.got(base + z)

    def z_out(self):
        t = self.t
        self.send(ACROSS, self.p_sum(1 - t.z), t.place(dz=1))

    def z_in(self):
        t = self.t
        self.result[:, HALF * self.half : HALF * (self.half + 1)] = self.p_sum(t.z) + self.got(ACROSS)

    def close(self):
        def step(slot, carry):
            self.copy(slot, self.t.place(dz=1)).wait_send()
            return carry

        lax.fori_loop(0, SLOTS, step, 0)


V = pltpu.VMEM
DMA = pltpu.SemaphoreType.DMA

SCRATCH = {
    "step": V((H, T), f32), "r": V((H, T), f32), "step_t": V((T, H), f32), "r_t": V((T, H), f32),
    "keep_t": V((NB, 1, H), f32), "skips": V((1, HP), f32),
    "within": V((T, HP), f32), "er": V((T, HP), f32), "xw": V((T, HP), bf16),
    "sl": V((NB + 1, N, HP), f32), "pd": V((NB + 1, 1, HP), f32), "st": V((N, HP), f32),
    "y": V((T, HP), f32), "normed": V((T, HP), bf16), "dn": V((T, HP), f32), "d_y": V((T, HP), f32),
    "row_own": V((H, T), f32), "row_carried": V((H, T), f32), "s1": V((H, T), f32), "s2": V((H, T), f32), "s3": V((H, T), f32),
    "gl": V((NB, N, HP), f32), "qd": V((NB, 1, HP), f32),
    "entering": V((N, HP), f32),
    "ds": V((NB, N, N), bf16), "ge": V((2, N, HP), bf16), "gy": V((2, N, HP), bf16), "psi": V((NB, 8, HP), f32),
    "wbuf": V((2, SEQ, SHARD, HALF), bf16), "cbuf": V((4, T, HP), bf16),
    "ws": DMA((2, 31)), "wr": DMA((2, SEQ)), "cs": DMA((6,)), "cr": DMA((4, 2)), "local": DMA((3,)),
    "out": V((2, SLOTS, SHARD, HALF), bf16), "inn": V((2, SLOTS, SHARD, HALF), bf16),
    "ss": DMA((2, SLOTS)), "rs": DMA((2, SLOTS)), "acc": V((2, 2, 4, SHARD, HALF), f32),
}


def multiply(cots, ws, out):
    def step(i, carry):
        half, tile = lax.div(i, 2), lax.rem(i, 2)
        at = pl.ds(pl.multiple_of(tile * 256, 256), 256)
        total = None
        for k in range(4):
            rows = ws[half, 8 * k : 8 * k + 8, :, at].reshape(1024, 256)
            term = dot(cots[k], rows)
            total = term if total is None else total + term
        out[:, pl.ds(pl.multiple_of(i * 256, 256), 256)] = total
        return carry

    lax.fori_loop(0, 4, step, 0)


def kernel(x, z, bm, cm, dt, bias, alog, skip, gain, resets, w, cot, d_x, d_z, d_b, d_c, d_dt, d_w, *refs):
    count = len(SCRATCH)
    s = dict(zip(SCRATCH, refs[:count]))
    swap = refs[count:]
    me = lax.axis_index("seq")
    step, r, step_t, r_t, keep_t, skips = (s[k] for k in ("step", "r", "step_t", "r_t", "keep_t", "skips"))
    within, er, xw, sl, pd, st, y = (s[k] for k in ("within", "er", "xw", "sl", "pd", "st", "y"))
    normed, dn, d_y, gl, qd = (s[k] for k in ("normed", "dn", "d_y", "gl", "qd"))
    entering, cbuf, wbuf, gt = s["entering"], s["cbuf"], s["wbuf"], st

    heads = Heads(cbuf, s["cs"], s["cr"])
    gathers = [Gather(h, wbuf, s["ws"], s["wr"]) for h in (0, 1)]

    def part(half, shard):
        block, at = lax.div(shard, 8), lax.rem(shard, 8)
        cols = pl.ds(pl.multiple_of(at * SHARD, SHARD), SHARD)
        return dot(cbuf[block, :, cols], normed[:, HALF * half : HALF * (half + 1)], TN)

    scatters = [Scatter(h, part, s["out"], s["inn"], s["ss"], s["rs"], s["acc"], d_w) for h in (0, 1)]

    def gather(name, *args):
        for g in gathers:
            getattr(g, name)(*args)

    def scatter(*names):
        for name in names:
            for g in scatters:
                getattr(g, name)()

    def block(b):
        forward_block(b, x, bm, cm, r, r_t, step_t, keep_t, within, er, xw, sl, pd, st)

    local = s["local"]
    mine = [pltpu.make_async_copy(w.at[:, pl.ds(HALF * h, HALF)], wbuf.at[h, me], local.at[h]) for h in (0, 1)]
    mine.append(pltpu.make_async_copy(cot, cbuf.at[heads.h], local.at[2]))
    for copy in mine:
        copy.start()
    for copy in mine:
        copy.wait()
    greet(me, [heads.core, heads.chip])

    gather("own")
    heads.own()
    prepare(dt, bias, alog, resets, skip, step, r, step_t, r_t, keep_t, skips)
    forward_start(pd, st)
    block(0)
    gather("across")
    block(1)
    gather("near")
    block(2)
    gather("far")
    block(3)
    sl[NB] = st[...]
    exchange_out(me, st, pd[NB], *swap[:4])
    gather("pass_on", (0,))
    heads.across()
    exchange_fold(me, False, *swap)
    gather("pass_on", (1,))
    exchange_in(me, entering, *swap)
    enter(x, cm, sl, pd, entering, er, skips, within, y)
    gather("pass_on", (2,))
    norm(y, z, gain, normed)
    gather("pass_on", (3,))
    heads.rest()
    scatter("q_far")
    gather("rest")
    scatter("q_near")
    multiply(cbuf, wbuf, dn)
    scatter("q_pass")
    unnorm(y, within, x, z, gain, skips, dn, d_z, d_y)
    scatter("q_own")
    gather_heads(y, s["row_own"])
    gather_heads(dn, s["row_carried"])
    state_grad(cm, r_t, keep_t, er, d_y, gl, qd, gt)
    exchange_out(me, gt, pd[NB], *swap[:4])
    scatter("p_far")
    backward_within(x, bm, cm, r, r_t, step_t, d_y, dn, s["ds"])
    exchange_fold(me, True, *swap)
    scatter("p_near", "p_own", "z_out")
    exchange_in(me, entering, *swap)
    backward_rest(x, bm, cm, r_t, step_t, skips, d_y, dn, s["ds"], xw, er, sl, gl, qd, entering, s["ge"], s["gy"], s["psi"], y, d_x, d_b, d_c)
    gather_heads(y, s["s1"])
    gather_heads(dn, s["s2"])
    gather_heads(d_y, s["s3"])
    steps_grad(dt, bias, alog, step, s["psi"], s["row_own"], s["row_carried"], s["s1"], s["s2"], s["s3"], d_dt)
    scatter("z_in", "close")
    gather("close")
    heads.close()


def body(x, z, bm, cm, dt, bias, alog, skip, gain, resets, w, cot):
    outs = [((T, HP), bf16), ((T, HP), bf16), ((T, N), bf16), ((T, N), bf16), ((H, T), f32), ((SHARD, HP), f32)]
    vmem = pl.BlockSpec(memory_space=pltpu.VMEM)
    return pl.pallas_call(
        kernel,
        out_shape=[jax.ShapeDtypeStruct(shape, kind) for shape, kind in outs],
        in_specs=[vmem] * 10 + [pl.BlockSpec(memory_space=pl.ANY)] * 2,
        out_specs=[vmem] * len(outs),
        scratch_shapes=list(SCRATCH.values()) + EXCHANGE,
        compiler_params=pltpu.CompilerParams(vmem_limit_bytes=63 << 20, collective_id=0, has_side_effects=True),
    )(x, z, bm, cm, dt, bias[None], alog[None], skip[None], gain[None], resets, w, cot)


def solution(mesh):
    s, h = P("seq", "head"), P("head")
    return jax.shard_map(
        body,
        mesh=mesh,
        in_specs=(s, s, s, s, P("head", "seq"), h, h, h, h, P("head", "seq"), s, s),
        out_specs=(s, s, s, s, P("head", "seq"), s),
        check_vma=False,
    )
```

```python
import jax
import jax.numpy as jnp
from jax import lax
from jax.experimental import pallas as pl
from jax.experimental.pallas import tpu as pltpu
from jax.sharding import PartitionSpec as P

T = 512
N = 128
HP = 1024
H = 16
NB = T // N
NP = HP // N
SEQ = 32

f32 = jnp.float32
bf16 = jnp.bfloat16
HI = lax.Precision.HIGHEST
NN = (((1,), (0,)), ((), ()))
NT = (((1,), (1,)), ((), ()))
TN = (((0,), (0,)), ((), ()))
OFF = -1e30


def dot(a, b, dims=NN, precision=None):
    return lax.dot_general(a, b, dims, precision=precision, preferred_element_type=f32)


def iota(shape, axis):
    return lax.broadcasted_iota(jnp.int32, shape, axis)


def pair_of(ref, rows, j, count):
    first = jnp.broadcast_to(ref[rows, 2 * j : 2 * j + 1], (count, N))
    second = jnp.broadcast_to(ref[rows, 2 * j + 1 : 2 * j + 2], (count, N))
    return jnp.where(iota((count, N), 1) < 64, first, second), first, second


def head_rows():
    row, col = iota((H, HP), 0), iota((H, HP), 1)
    return ((col >= 64 * row) & (col < 64 * row + 64)).astype(bf16)


def halves(value):
    high = value.astype(bf16)
    return high, (value - high.astype(f32)).astype(bf16)


def head_sums(value):
    high, low = halves(value)
    ones = head_rows()
    return dot(ones, high, NT) + dot(ones, low, NT)


def stacked(value):
    low = iota(value.shape, 1) < 64
    zero = jnp.zeros_like(value)
    return jnp.concatenate([jnp.where(low, value, zero), jnp.where(low, zero, value)], axis=0)


def lanes(j):
    return slice(N * j, N * j + N)


def column(ref):
    eye = iota((H, H), 0) == iota((H, H), 1)
    return jnp.sum(jnp.where(eye, jnp.broadcast_to(ref[...], (H, H)), 0.0), axis=1, keepdims=True)


def prepare(dt, bias, alog, resets, skip, step, r, step_t, r_t, keep_t, skips):
    raw = dt[...] + column(bias)
    step[...] = jnp.maximum(raw, 0.0) + jnp.log1p(jnp.exp(-jnp.abs(raw)))
    rate = -step[...] * jnp.exp(column(alog))
    keep = 1.0 - resets[...].astype(f32)
    square = iota((H, H), 0) == iota((H, H), 1)
    for b in range(NB):
        spread = jnp.where(square, jnp.broadcast_to(keep[:, b : b + 1], (H, H)), 0.0)
        keep_t[b] = jnp.sum(spread, axis=0, keepdims=True)
    for j in range(NP):
        skips[:, lanes(j)] = pair_of(skip, slice(0, 1), j, 1)[0]
    row, col = iota((N, N), 0), iota((N, N), 1)
    upper = (row <= col).astype(f32)
    eye = (row == col).astype(f32)
    for b in range(NB):
        at = lanes(b)
        r[:, at] = dot(rate[:, at], upper, precision=HI)
        r_t[at, :] = dot(eye, r[:, at], NT, HI)
        step_t[at, :] = dot(eye, step[:, at], NT, HI)


def forward_block(b, x, bm, cm, r, r_t, step_t, keep_t, within, er, xw, sl, pd, st):
    base = b * N
    rows = pl.ds(base, N)
    mask = iota((N, N), 0) >= iota((N, N), 1)
    b_blk, c_blk = bm[rows, :], cm[rows, :]
    b_flip = b_blk.astype(f32).T.astype(bf16)
    scores = dot(c_blk, b_blk, NT)
    for j in range(NP):
        at = lanes(j)
        run, run0, run1 = pair_of(r_t, rows, j, N)
        size = pair_of(step_t, rows, j, N)[0]
        last = pair_of(r_t, pl.ds(base + N - 1, 1), j, 1)[0]
        keep = pair_of(keep_t.at[b], slice(0, 1), j, 1)[0]
        mixing = [
            (jnp.exp(jnp.where(mask, col - r[2 * j + k : 2 * j + k + 1, rows], OFF)) * scores).astype(bf16)
            for k, col in enumerate((run0, run1))
        ]
        x_val = x[rows, at].astype(f32)
        sized = x_val * size
        within[rows, at] = dot(jnp.concatenate(mixing, axis=1), stacked(sized.astype(bf16)))
        er[rows, at] = jnp.exp(run)
        weighted = (sized * jnp.exp(last - run)).astype(bf16)
        xw[rows, at] = weighted
        state = st[:, at] * keep
        sl[b, :, at] = state
        span = pd[b, :, at] * keep
        pd[b, :, at] = span
        decay = jnp.exp(last)
        pd[b + 1, :, at] = span * decay
        st[:, at] = state * decay + dot(b_flip, weighted)


def forward_start(pd, st):
    st[...] = jnp.zeros_like(st)
    pd[0] = jnp.ones((1, HP), f32)


def enter(x, cm, sl, pd, entering, er, skip, within, y):
    def step(b, carry):
        rows = pl.ds(pl.multiple_of(b * N, N), N)
        c_blk = cm[rows, :]
        for j in range(NP):
            at = lanes(j)
            state = sl[b, :, at] + pd[b, :, at] * entering[:, at]
            sl[b, :, at] = state
            high, low = halves(state)
            y[rows, at] = within[rows, at] + (dot(c_blk, high) + dot(c_blk, low)) * er[rows, at] + skip[:, at] * x[rows, at].astype(f32)
        return carry

    lax.fori_loop(0, NB, step, 0)


CH = 32


def norm(y, z, gain, normed):
    def step(i, carry):
        rows = pl.ds(pl.multiple_of(i * CH, CH), CH)
        z_val = z[rows, :].astype(f32)
        gated = y[rows, :] * (z_val / (1.0 + jnp.exp(-z_val)))
        factor = lax.rsqrt(jnp.mean(gated * gated, axis=1, keepdims=True) + 1e-05)
        normed[rows, :] = (gated * factor * gain[...]).astype(bf16)
        return carry

    lax.fori_loop(0, T // CH, step, 0)


def unnorm(y, within, x, z, gain, skip, d_normed, d_z, d_y):
    def step(i, carry):
        rows = pl.ds(pl.multiple_of(i * CH, CH), CH)
        z_val = z[rows, :].astype(f32)
        y_val = y[rows, :]
        sig = 1.0 / (1.0 + jnp.exp(-z_val))
        silu = z_val * sig
        gated = y_val * silu
        factor = lax.rsqrt(jnp.mean(gated * gated, axis=1, keepdims=True) + 1e-05)
        scaled = d_normed[rows, :] * gain[...]
        along = jnp.mean(scaled * gated, axis=1, keepdims=True)
        d_gated = factor * scaled - gated * (factor * factor * factor * along)
        d_z[rows, :] = (d_gated * y_val * (sig * (1.0 + z_val * (1.0 - sig)))).astype(bf16)
        d_mixed = d_gated * silu
        d_y[rows, :] = d_mixed
        own = within[rows, :]
        y[rows, :] = d_mixed * own
        d_normed[rows, :] = d_mixed * (y_val - skip[...] * x[rows, :].astype(f32) - own)
        return carry

    lax.fori_loop(0, T // CH, step, 0)


def gather_heads(work, sums):
    def step(b, carry):
        rows = pl.ds(pl.multiple_of(b * N, N), N)
        sums[:, rows] = head_sums(work[rows, :])
        return carry

    lax.fori_loop(0, NB, step, 0)


def state_grad(cm, r_t, keep_t, er, d_y, gl, qd, gt):
    gt[...] = jnp.zeros_like(gt)
    qd[NB - 1] = jnp.ones((1, HP), f32)

    def step(i, carry):
        b = NB - 1 - i
        base = pl.multiple_of(b * N, N)
        rows = pl.ds(base, N)
        c_flip = cm[rows, :].astype(f32).T.astype(bf16)
        for j in range(NP):
            at = lanes(j)
            last = pair_of(r_t, pl.ds(base + N - 1, 1), j, 1)[0]
            keep = pair_of(keep_t.at[b], slice(0, 1), j, 1)[0]
            high, low = halves(er[rows, at] * d_y[rows, at])
            grad = gt[:, at]
            gl[b, :, at] = grad
            decay = jnp.exp(last)
            gt[:, at] = keep * (decay * grad + dot(c_flip, high) + dot(c_flip, low))
            value = qd[b, :, at]

            @pl.when(b > 0)
            def _():
                qd[b - 1, :, at] = keep * decay * value

        return carry

    lax.fori_loop(0, NB, step, 0)


def backward_within(x, bm, cm, r, r_t, step_t, d_y, v, ds):
    def step(b, carry):
        rows = pl.ds(pl.multiple_of(b * N, N), N)
        mask = iota((N, N), 0) <= iota((N, N), 1)
        scores = dot(bm[rows, :], cm[rows, :], NT)
        total = jnp.zeros((N, N), f32)
        for j in range(NP):
            at = lanes(j)
            run0 = jnp.broadcast_to(r_t[rows, 2 * j : 2 * j + 1], (N, N))
            run1 = jnp.broadcast_to(r_t[rows, 2 * j + 1 : 2 * j + 2], (N, N))
            size = pair_of(step_t, rows, j, N)[0]
            decays = [
                jnp.exp(jnp.where(mask, r[2 * j + k : 2 * j + k + 1, rows] - col, OFF))
                for k, col in enumerate((run0, run1))
            ]
            high, low = halves(d_y[rows, at])
            mixing = jnp.concatenate([(decay * scores).astype(bf16) for decay in decays], axis=1)
            v[rows, at] = dot(mixing, stacked(high)) + dot(mixing, stacked(low))
            sized = (x[rows, at].astype(f32) * size).astype(bf16)
            both = stacked(sized)
            product = dot(both, high, NT) + dot(both, low, NT)
            total = total + product[:N] * decays[0] + product[N:] * decays[1]
        ds[b] = total.astype(bf16)
        return carry

    lax.fori_loop(0, NB, step, 0)


def backward_rest(span, x, bm, cm, r_t, step_t, skip, d_y, v, ds, xw, er, sl, gl, qd, arriving, ge, gy, psi, own, d_x, d_b, d_c):
    def step(b, carry):
        base = pl.multiple_of(b * N, N)
        rows = pl.ds(base, N)
        b_blk, c_blk = bm[rows, :], cm[rows, :]
        for j in range(NP):
            at = lanes(j)
            run = pair_of(r_t, rows, j, N)[0]
            size = pair_of(step_t, rows, j, N)[0]
            last = pair_of(r_t, pl.ds(base + N - 1, 1), j, 1)[0]
            grad = gl[b, :, at] + qd[b, :, at] * arriving[:, at]
            passing = grad * sl[b, :, at]
            psi[b, :, at] = jnp.exp(last) * jnp.sum(passing.reshape(N // 8, 8, N), axis=0)
            high, low = halves(grad)
            ge[0, :, at] = high
            ge[1, :, at] = low
            local = v[rows, at]
            gy[0, :, at], gy[1, :, at] = halves(er[rows, at] * d_y[rows, at])
            reach = dot(b_blk, high) + dot(b_blk, low)
            carried = jnp.exp(last - run) * reach
            x_val = x[rows, at].astype(f32)
            sized = x_val * size
            d_x[rows, at] = (size * (local + carried) + skip[:, at] * d_y[rows, at]).astype(bf16)
            own[rows, at] = sized.astype(bf16).astype(f32) * local
            v[rows, at] = xw[rows, at].astype(f32) * reach
            d_y[rows, at] = x_val * (local + carried)
        d_b[rows, :] = (dot(ds[b], c_blk) + dot(xw[rows, :], ge[0], NT) + dot(xw[rows, :], ge[1], NT)).astype(bf16)
        late = sl[b].astype(bf16)
        d_c[rows, :] = (dot(ds[b], b_blk, TN) + dot(gy[0], late, NT) + dot(gy[1], late, NT)).astype(bf16)
        return carry

    lax.fori_loop(*span, step, 0)


def steps_grad(dt, bias, alog, step, psi, row_own, row_carried, own, carried, whole, out):
    row, col = iota((N, N), 0), iota((N, N), 1)
    since = (row >= col).astype(f32)
    before = (row < col).astype(f32)
    raw = dt[...] + column(bias)
    sig = 1.0 / (1.0 + jnp.exp(-raw))
    pull = jnp.exp(column(alog))
    ones = head_rows().astype(f32)
    for b in range(NB):
        at = lanes(b)
        past = jnp.sum(dot(ones, psi[b], NT, HI), axis=1, keepdims=True)
        d_rate = dot(row_own[:, at] - own[:, at] + row_carried[:, at], since, precision=HI) + past
        d_rate = d_rate + dot(carried[:, at], before, precision=HI)
        out[:, at] = (whole[:, at] - pull * d_rate) * sig[:, at]


MESH = pl.DeviceIdType.MESH
SHARD = 128
HALF = HP // 2
D = 4096


def mod(value, size):
    return lax.rem(value + size, size)


def greet(me, heads):
    barrier = pltpu.get_barrier_semaphore()

    def step(k, carry):
        pl.semaphore_signal(barrier, inc=1, device_id={"seq": lax.rem(me + k, SEQ)}, device_id_type=MESH)
        return carry

    lax.fori_loop(1, SEQ, step, 0)
    for h in heads:
        pl.semaphore_signal(barrier, inc=1, device_id={"head": h}, device_id_type=MESH)
    pl.semaphore_wait(barrier, SEQ - 1 + len(heads))


def remote(src, dst, ssem, rsem, **device):
    return pltpu.make_async_remote_copy(
        src_ref=src, dst_ref=dst, send_sem=ssem, recv_sem=rsem, device_id=device, device_id_type=MESH
    )


SLICE = 32


def each_other(me, fn):
    def step(k, carry):
        fn(lax.rem(me + k, SEQ))
        return carry

    lax.fori_loop(1, SEQ, step, 0)


def to_copy(me, rows, buf, land, ssem, rsem, other):
    return remote(buf.at[other, :rows], land.at[me, :rows], ssem.at[other], rsem.at[me], seq=other)


def from_copy(me, rows, buf, land, ssem, rsem, other):
    return remote(buf.at[me, :rows], land.at[other, :rows], ssem.at[me], rsem.at[other], seq=other)


def exchange_out(me, state, decay, out1, in1, s1, r1):
    rows = SLICE if decay is None else SLICE + 8
    for j in range(NP):
        for i in range(N // SLICE):
            k = j * (N // SLICE) + i
            out1[k, :SLICE] = state[SLICE * i : SLICE * (i + 1), lanes(j)]
            if decay is not None:
                out1[k, SLICE:] = jnp.broadcast_to(decay[:, lanes(j)], (8, N))
    each_other(me, lambda o: to_copy(me, rows, out1, in1, s1, r1, o).start())
    in1[me, :rows] = out1[me, :rows]


def exchange_fold(me, backward, out1, in1, s1, r1, out2, in2, s2, r2):
    rows = SLICE if backward else SLICE + 8
    each_other(me, lambda o: from_copy(me, rows, out1, in1, s1, r1, o).wait_recv())

    def step(i, total):
        at = SEQ - 1 - i if backward else i
        out2[at] = total
        return total * in1[at, SLICE : SLICE + 1] + in1[at, :SLICE]

    lax.fori_loop(0, SEQ, step, jnp.zeros((SLICE, N), f32))
    each_other(me, lambda o: to_copy(me, SLICE, out2, in2, s2, r2, o).start())
    in2[me] = out2[me]


def exchange_in(me, backward, result, out1, in1, s1, r1, out2, in2, s2, r2):
    rows = SLICE if backward else SLICE + 8
    each_other(me, lambda o: from_copy(me, SLICE, out2, in2, s2, r2, o).wait_recv())
    for j in range(NP):
        for i in range(N // SLICE):
            result[SLICE * i : SLICE * (i + 1), lanes(j)] = in2[j * (N // SLICE) + i]

    def done(o):
        to_copy(me, rows, out1, in1, s1, r1, o).wait_send()
        to_copy(me, SLICE, out2, in2, s2, r2, o).wait_send()

    each_other(me, done)


EXCHANGE = [
    pltpu.VMEM((SEQ, SLICE + 8, N), f32),
    pltpu.VMEM((SEQ, SLICE + 8, N), f32),
    pltpu.SemaphoreType.DMA((SEQ,)),
    pltpu.SemaphoreType.DMA((SEQ,)),
    pltpu.VMEM((SEQ, SLICE, N), f32),
    pltpu.VMEM((SEQ, SLICE, N), f32),
    pltpu.SemaphoreType.DMA((SEQ,)),
    pltpu.SemaphoreType.DMA((SEQ,)),
]


class Torus:
    def __init__(self, half):
        self.half = half
        me = lax.axis_index("seq")
        x, y = lax.rem(me, 4), lax.rem(lax.div(me, 4), 4)
        self.z = lax.div(me, 16)
        self.p, self.q = (x, y) if half == 0 else (y, x)

    def at(self, z, p, q):
        return z * 16 + (q * 4 + p if self.half == 0 else p * 4 + q)

    def place(self, dz=0, dp=0, dq=0):
        z = 1 - self.z if dz else self.z
        return self.at(z, mod(self.p + dp, 4), mod(self.q + dq, 4))


class Gather:
    def __init__(self, half, buf, ssem, rsem):
        self.t, self.half, self.buf, self.ssem, self.rsem, self.n = Torus(half), half, buf, ssem, rsem, 0
        self.sent = []

    def copy(self, shard, to, index):
        ref = self.buf.at[self.half, shard]
        return remote(ref, ref, self.ssem.at[self.half, index], self.rsem.at[self.half, shard], seq=to)

    def send(self, shard, to):
        copy = self.copy(shard, to, self.n)
        copy.start()
        self.sent.append(copy)
        self.n += 1

    def wait(self, shard):
        self.copy(shard, self.t.place(dz=1), 0).wait_recv()

    def spread(self, shard):
        self.send(shard, self.t.place(dq=1))
        self.send(shard, self.t.place(dq=-1))

    def own(self):
        t = self.t
        mine = t.place()
        self.send(mine, t.place(dz=1))
        self.send(mine, t.place(dp=1))
        self.send(mine, t.place(dp=-1))
        self.spread(mine)

    def across(self):
        t = self.t
        other = t.place(dz=1)
        self.wait(other)
        self.send(other, t.place(dp=1))
        self.send(other, t.place(dp=-1))
        self.spread(other)

    def near(self):
        t = self.t
        for z in (0, 1):
            for dp in (-1, 1):
                shard = t.at(z, mod(t.p + dp, 4), t.q)
                self.wait(shard)
                if (z, dp) in ((0, -1), (1, 1)):
                    self.send(shard, t.place(dp=-dp))
                self.spread(shard)

    def far(self):
        t = self.t
        for z in (0, 1):
            shard = t.at(z, mod(t.p + 2, 4), t.q)
            self.wait(shard)
            self.spread(shard)

    def pass_on(self, ks):
        t = self.t
        for k in ks:
            p = mod(t.p + (0, 1, 3, 2)[k], 4)
            for z, dq in ((0, -1), (1, 1)):
                shard = t.at(z, p, mod(t.q + dq, 4))
                self.wait(shard)
                self.send(shard, t.place(dq=-dq))

    def rest(self, ends):
        t = self.t
        for p in range(4):
            for z, dq in ends:
                self.wait(t.at(z, p, mod(t.q + dq, 4)))

    def multiply(self, cots, out, dqs, first):
        t = self.t
        at = slice(HALF * self.half, HALF * (self.half + 1))
        total = None if first else out[:, at]
        for dq in dqs:
            for p in range(4):
                pair = [t.at(z, p, mod(t.q + dq, 4)) for z in (0, 1)]
                left = [
                    cots[lax.div(k, 8), :, pl.ds(pl.multiple_of(lax.rem(k, 8) * SHARD, SHARD), SHARD)] for k in pair
                ]
                right = [self.buf[self.half, k] for k in pair]
                term = dot(jnp.concatenate(left, axis=1), jnp.concatenate(right, axis=0))
                total = term if total is None else total + term
        out[:, at] = total

    def close(self):
        for copy in self.sent:
            copy.wait_send()


class Heads:
    PARTS = 2

    def __init__(self, buf, ssem, rsem):
        self.h = lax.axis_index("head")
        self.core = self.h + 1 - 2 * lax.rem(self.h, 2)
        self.chip = lax.rem(self.h + 2, 4)
        self.buf, self.ssem, self.rsem, self.sent = buf, ssem, rsem, []

    def copy(self, block, part, to, index):
        ref = self.buf.at[block, pl.ds(part * (T // self.PARTS), T // self.PARTS)]
        return remote(ref, ref, self.ssem.at[index], self.rsem.at[block, part], head=to)

    def send(self, block, part, to):
        copy = self.copy(block, part, to, len(self.sent))
        copy.start()
        self.sent.append(copy)

    def own(self):
        for part in range(self.PARTS):
            self.send(self.h, part, self.chip)
        for part in range(self.PARTS):
            self.send(self.h, part, self.core)

    def across(self):
        for part in range(self.PARTS):
            self.copy(self.chip, part, self.chip, 0).wait_recv()
            self.send(self.chip, part, self.core)

    def rest(self):
        for part in range(self.PARTS):
            self.copy(self.core, part, self.core, 0).wait_recv()
            self.copy(lax.rem(self.core + 2, 4), part, self.core, 0).wait_recv()

    def close(self):
        for copy in self.sent:
            copy.wait_send()


FARP, FARM, NEARP, NEARM, PFARP, PFARM, PNEARP, PNEARM, ACROSS = 0, 4, 8, 16, 24, 25, 26, 28, 30
SLOTS = 31


class Scatter:
    def __init__(self, half, part, out, inn, ssem, rsem, acc, result):
        self.t, self.half, self.part, self.out, self.inn = Torus(half), half, part, out, inn
        self.ssem, self.rsem, self.acc, self.result = ssem, rsem, acc, result

    def copy(self, slot, to):
        h = self.half
        return remote(self.out.at[h, slot], self.inn.at[h, slot], self.ssem.at[h, slot], self.rsem.at[h, slot], seq=to)

    def send(self, slot, value, to):
        self.out[self.half, slot] = value.astype(bf16)
        self.copy(slot, to).start()

    def got(self, slot):
        self.copy(slot, self.t.place(dz=1)).wait_recv()
        return self.inn[self.half, slot].astype(f32)

    def loop(self, fn):
        def step(i, carry):
            fn(lax.rem(self.t.p + 2 + 3 * i + 3 * lax.div(i * (i - 1), 2), 4))
            return carry

        lax.fori_loop(0, 4, step, 0)

    def q_far(self):
        t = self.t
        far = mod(t.q + 2, 4)

        def fn(p):
            self.send(FARP + p, self.part(self.half, t.at(0, p, far)), t.place(dq=1))
            self.send(FARM + p, self.part(self.half, t.at(1, p, far)), t.place(dq=-1))

        self.loop(fn)

    def q_near(self):
        t = self.t
        up, down = mod(t.q + 1, 4), mod(t.q - 1, 4)

        def fn(p):
            self.send(NEARP + 4 + p, self.part(self.half, t.at(1, p, up)), t.place(dq=1))
            self.send(NEARM + p, self.part(self.half, t.at(0, p, down)), t.place(dq=-1))

        self.loop(fn)

    def q_pass(self):
        t = self.t
        up, down = mod(t.q + 1, 4), mod(t.q - 1, 4)

        def fn(p):
            self.send(NEARP + p, self.part(self.half, t.at(0, p, up)) + self.got(FARP + p), t.place(dq=1))
            self.send(NEARM + 4 + p, self.part(self.half, t.at(1, p, down)) + self.got(FARM + p), t.place(dq=-1))

        self.loop(fn)

    def q_own(self):
        t = self.t

        def fn(p):
            for z in (0, 1):
                self.acc[self.half, z, p] = self.part(self.half, t.at(z, p, t.q))

        self.loop(fn)

    def total(self, z, p):
        return self.acc[self.half, z, p] + self.got(NEARP + 4 * z + p) + self.got(NEARM + 4 * z + p)

    def p_far(self):
        t = self.t
        far = mod(t.p + 2, 4)
        self.send(PFARP, self.total(0, far), t.place(dp=1))
        self.send(PFARM, self.total(1, far), t.place(dp=-1))

    def p_near(self):
        t = self.t
        up, down = mod(t.p + 1, 4), mod(t.p - 1, 4)
        self.send(PNEARP + 1, self.total(1, up), t.place(dp=1))
        self.send(PNEARM, self.total(0, down), t.place(dp=-1))
        self.send(PNEARP, self.total(0, up) + self.got(PFARP), t.place(dp=1))
        self.send(PNEARM + 1, self.total(1, down) + self.got(PFARM), t.place(dp=-1))

    def p_own(self):
        t = self.t
        for z in (0, 1):
            self.acc[self.half, z, t.p] = self.total(z, t.p)

    def p_sum(self, z):
        return self.acc[self.half, z, self.t.p] + self.got_at(PNEARP, z) + self.got_at(PNEARM, z)

    def got_at(self, base, z):
        return self.got(base + z)

    def z_out(self):
        t = self.t
        self.send(ACROSS, self.p_sum(1 - t.z), t.place(dz=1))

    def z_in(self):
        t = self.t
        self.result[:, HALF * self.half : HALF * (self.half + 1)] = self.p_sum(t.z) + self.got(ACROSS)

    def close(self):
        def step(slot, carry):
            self.copy(slot, self.t.place(dz=1)).wait_send()
            return carry

        lax.fori_loop(0, SLOTS, step, 0)


V = pltpu.VMEM
DMA = pltpu.SemaphoreType.DMA

SCRATCH = {
    "step": V((H, T), f32), "r": V((H, T), f32), "step_t": V((T, H), f32), "r_t": V((T, H), f32),
    "keep_t": V((NB, 1, H), f32), "skips": V((1, HP), f32),
    "within": V((T, HP), f32), "er": V((T, HP), f32), "xw": V((T, HP), bf16),
    "sl": V((NB + 1, N, HP), f32), "pd": V((NB + 1, 1, HP), f32), "st": V((N, HP), f32),
    "y": V((T, HP), f32), "normed": V((T, HP), bf16), "dn": V((T, HP), f32), "d_y": V((T, HP), f32),
    "row_own": V((H, T), f32), "row_carried": V((H, T), f32), "s1": V((H, T), f32), "s2": V((H, T), f32), "s3": V((H, T), f32),
    "gl": V((NB, N, HP), f32), "qd": V((NB, 1, HP), f32),
    "entering": V((N, HP), f32),
    "ds": V((NB, N, N), bf16), "ge": V((2, N, HP), bf16), "gy": V((2, N, HP), bf16), "psi": V((NB, 8, HP), f32),
    "wbuf": V((2, SEQ, SHARD, HALF), bf16), "cbuf": V((4, T, HP), bf16),
    "ws": DMA((2, 31)), "wr": DMA((2, SEQ)), "cs": DMA((6,)), "cr": DMA((4, 2)), "local": DMA((3,)),
    "out": V((2, SLOTS, SHARD, HALF), bf16), "inn": V((2, SLOTS, SHARD, HALF), bf16),
    "ss": DMA((2, SLOTS)), "rs": DMA((2, SLOTS)), "acc": V((2, 2, 4, SHARD, HALF), f32),
}


def kernel(x, z, bm, cm, dt, bias, alog, skip, gain, resets, w, cot, d_x, d_z, d_b, d_c, d_dt, d_w, *refs):
    count = len(SCRATCH)
    s = dict(zip(SCRATCH, refs[:count]))
    swap = refs[count:]
    me = lax.axis_index("seq")
    step, r, step_t, r_t, keep_t, skips = (s[k] for k in ("step", "r", "step_t", "r_t", "keep_t", "skips"))
    within, er, xw, sl, pd, st, y = (s[k] for k in ("within", "er", "xw", "sl", "pd", "st", "y"))
    normed, dn, d_y, gl, qd = (s[k] for k in ("normed", "dn", "d_y", "gl", "qd"))
    entering, cbuf, wbuf, gt = s["entering"], s["cbuf"], s["wbuf"], st

    heads = Heads(cbuf, s["cs"], s["cr"])
    gathers = [Gather(h, wbuf, s["ws"], s["wr"]) for h in (0, 1)]

    def part(half, shard):
        block, at = lax.div(shard, 8), lax.rem(shard, 8)
        cols = pl.ds(pl.multiple_of(at * SHARD, SHARD), SHARD)
        return dot(cbuf[block, :, cols], normed[:, HALF * half : HALF * (half + 1)], TN)

    scatters = [Scatter(h, part, s["out"], s["inn"], s["ss"], s["rs"], s["acc"], d_w) for h in (0, 1)]

    def gather(name, *args):
        for g in gathers:
            getattr(g, name)(*args)

    def scatter(*names):
        for name in names:
            for g in scatters:
                getattr(g, name)()

    def block(b):
        forward_block(b, x, bm, cm, r, r_t, step_t, keep_t, within, er, xw, sl, pd, st)

    local = s["local"]
    mine = [pltpu.make_async_copy(w.at[:, pl.ds(HALF * h, HALF)], wbuf.at[h, me], local.at[h]) for h in (0, 1)]
    mine.append(pltpu.make_async_copy(cot, cbuf.at[heads.h], local.at[2]))
    for copy in mine:
        copy.start()
    greet(me, [heads.core, heads.chip])
    for copy in mine:
        copy.wait()

    gather("own")
    heads.own()
    prepare(dt, bias, alog, resets, skip, step, r, step_t, r_t, keep_t, skips)
    forward_start(pd, st)
    block(0)
    gather("across")
    block(1)
    gather("near")
    block(2)
    gather("far")
    block(3)
    sl[NB] = st[...]
    exchange_out(me, st, pd[NB], *swap[:4])
    gather("pass_on", (0,))
    heads.across()
    gather("pass_on", (1,))
    exchange_fold(me, False, *swap)
    gather("pass_on", (2,))
    heads.rest()
    gather("multiply", cbuf, dn, (0,), True)
    exchange_in(me, False, entering, *swap)
    gather("pass_on", (3,))
    enter(x, cm, sl, pd, entering, er, skips, within, y)
    norm(y, z, gain, normed)
    scatter("q_far")
    gather("rest", ((1, -1), (0, 1)))
    gather("multiply", cbuf, dn, (1, 3), False)
    scatter("q_near")
    gather("rest", ((0, 2), (1, 2)))
    gather("multiply", cbuf, dn, (2,), False)
    unnorm(y, within, x, z, gain, skips, dn, d_z, d_y)
    state_grad(cm, r_t, keep_t, er, d_y, gl, qd, gt)
    exchange_out(me, gt, None, *swap[:4])
    scatter("q_pass")
    gather_heads(dn, s["row_carried"])
    scatter("q_own")
    backward_within(x, bm, cm, r, r_t, step_t, d_y, dn, s["ds"])
    exchange_fold(me, True, *swap)
    scatter("p_far")
    gather_heads(y, s["row_own"])
    scatter("p_near")
    exchange_in(me, True, entering, *swap)
    late = (x, bm, cm, r_t, step_t, skips, d_y, dn, s["ds"], xw, er, sl, gl, qd, entering, s["ge"], s["gy"], s["psi"], y, d_x, d_b, d_c)
    backward_rest((0, 2), *late)
    scatter("p_own", "z_out")
    backward_rest((2, 4), *late)
    gather_heads(y, s["s1"])
    gather_heads(dn, s["s2"])
    gather_heads(d_y, s["s3"])
    steps_grad(dt, bias, alog, step, s["psi"], s["row_own"], s["row_carried"], s["s1"], s["s2"], s["s3"], d_dt)
    scatter("z_in", "close")
    gather("close")
    heads.close()


def finish(*refs):
    half = len(refs) // 2
    for source, target in zip(refs[:half], refs[half:]):
        target[...] = source[...]


def body(x, z, bm, cm, dt, bias, alog, skip, gain, resets, w, cot):
    outs = [((T, HP), bf16), ((T, HP), bf16), ((T, N), bf16), ((T, N), bf16), ((H, T), f32), ((SHARD, HP), f32)]
    vmem = pl.BlockSpec(memory_space=pltpu.VMEM)
    results = pl.pallas_call(
        kernel,
        out_shape=[jax.ShapeDtypeStruct(shape, kind) for shape, kind in outs],
        in_specs=[vmem] * 10 + [pl.BlockSpec(memory_space=pl.ANY)] * 2,
        out_specs=[vmem] * len(outs),
        scratch_shapes=list(SCRATCH.values()) + EXCHANGE,
        compiler_params=pltpu.CompilerParams(vmem_limit_bytes=63 << 20, collective_id=0, has_side_effects=True),
    )(x, z, bm, cm, dt, bias[None], alog[None], skip[None], gain[None], resets, w, cot)
    blocks = [pl.BlockSpec((shape[0] // 4, shape[1]), lambda i: (i, 0)) for shape, kind in outs]
    blocks[4] = pl.BlockSpec((H, T // 4), lambda i: (0, i))
    return pl.pallas_call(
        finish,
        grid=(4,),
        out_shape=[jax.ShapeDtypeStruct(shape, kind) for shape, kind in outs],
        in_specs=blocks,
        out_specs=blocks,
    )(*results)


def solution(mesh):
    s, h = P("seq", "head"), P("head")
    return jax.shard_map(
        body,
        mesh=mesh,
        in_specs=(s, s, s, s, P("head", "seq"), h, h, h, h, P("head", "seq"), s, s),
        out_specs=(s, s, s, s, P("head", "seq"), s),
        check_vma=False,
    )
```

```python
import jax
import jax.numpy as jnp
from jax import lax
from jax.experimental import pallas as pl
from jax.experimental.pallas import tpu as pltpu
from jax.sharding import PartitionSpec as P

T = 512
N = 128
HP = 1024
H = 16
NB = T // N
NP = HP // N
SEQ = 32

f32 = jnp.float32
bf16 = jnp.bfloat16
HI = lax.Precision.HIGHEST
NN = (((1,), (0,)), ((), ()))
NT = (((1,), (1,)), ((), ()))
TN = (((0,), (0,)), ((), ()))
OFF = -1e30


def dot(a, b, dims=NN, precision=None):
    return lax.dot_general(a, b, dims, precision=precision, preferred_element_type=f32)


def iota(shape, axis):
    return lax.broadcasted_iota(jnp.int32, shape, axis)


def pair_of(ref, rows, j, count):
    first = jnp.broadcast_to(ref[rows, 2 * j : 2 * j + 1], (count, N))
    second = jnp.broadcast_to(ref[rows, 2 * j + 1 : 2 * j + 2], (count, N))
    return jnp.where(iota((count, N), 1) < 64, first, second), first, second


def head_rows():
    row, col = iota((H, HP), 0), iota((H, HP), 1)
    return ((col >= 64 * row) & (col < 64 * row + 64)).astype(bf16)


def halves(value):
    high = value.astype(bf16)
    return high, (value - high.astype(f32)).astype(bf16)


def head_sums(value):
    high, low = halves(value)
    ones = head_rows()
    return dot(ones, high, NT) + dot(ones, low, NT)


def stacked(value):
    low = iota(value.shape, 1) < 64
    zero = jnp.zeros_like(value)
    return jnp.concatenate([jnp.where(low, value, zero), jnp.where(low, zero, value)], axis=0)


def lanes(j):
    return slice(N * j, N * j + N)


def column(ref):
    eye = iota((H, H), 0) == iota((H, H), 1)
    return jnp.sum(jnp.where(eye, jnp.broadcast_to(ref[...], (H, H)), 0.0), axis=1, keepdims=True)


def prepare(dt, bias, alog, resets, skip, step, r, step_t, r_t, keep_t, skips):
    raw = dt[...] + column(bias)
    step[...] = jnp.maximum(raw, 0.0) + jnp.log1p(jnp.exp(-jnp.abs(raw)))
    rate = -step[...] * jnp.exp(column(alog))
    keep = 1.0 - resets[...].astype(f32)
    square = iota((H, H), 0) == iota((H, H), 1)
    for b in range(NB):
        spread = jnp.where(square, jnp.broadcast_to(keep[:, b : b + 1], (H, H)), 0.0)
        keep_t[b] = jnp.sum(spread, axis=0, keepdims=True)
    for j in range(NP):
        skips[:, lanes(j)] = pair_of(skip, slice(0, 1), j, 1)[0]
    row, col = iota((N, N), 0), iota((N, N), 1)
    upper = (row <= col).astype(f32)
    eye = (row == col).astype(f32)
    for b in range(NB):
        at = lanes(b)
        r[:, at] = dot(rate[:, at], upper, precision=HI)
        r_t[at, :] = dot(eye, r[:, at], NT, HI)
        step_t[at, :] = dot(eye, step[:, at], NT, HI)


def forward_block(b, x, bm, cm, r, r_t, step_t, keep_t, within, er, xw, sl, pd, st):
    base = b * N
    rows = pl.ds(base, N)
    mask = iota((N, N), 0) >= iota((N, N), 1)
    b_blk, c_blk = bm[rows, :], cm[rows, :]
    b_flip = b_blk.astype(f32).T.astype(bf16)
    scores = dot(c_blk, b_blk, NT)
    for j in range(NP):
        at = lanes(j)
        run, run0, run1 = pair_of(r_t, rows, j, N)
        size = pair_of(step_t, rows, j, N)[0]
        last = pair_of(r_t, pl.ds(base + N - 1, 1), j, 1)[0]
        keep = pair_of(keep_t.at[b], slice(0, 1), j, 1)[0]
        mixing = [
            (jnp.exp(jnp.where(mask, col - r[2 * j + k : 2 * j + k + 1, rows], OFF)) * scores).astype(bf16)
            for k, col in enumerate((run0, run1))
        ]
        x_val = x[rows, at].astype(f32)
        sized = x_val * size
        within[rows, at] = dot(jnp.concatenate(mixing, axis=1), stacked(sized.astype(bf16)))
        er[rows, at] = jnp.exp(run)
        weighted = (sized * jnp.exp(last - run)).astype(bf16)
        xw[rows, at] = weighted
        state = st[:, at] * keep
        sl[b, :, at] = state
        span = pd[b, :, at] * keep
        pd[b, :, at] = span
        decay = jnp.exp(last)
        pd[b + 1, :, at] = span * decay
        st[:, at] = state * decay + dot(b_flip, weighted)


def forward_start(pd, st):
    st[...] = jnp.zeros_like(st)
    pd[0] = jnp.ones((1, HP), f32)


def enter(x, cm, sl, pd, entering, er, skip, within, y):
    def step(b, carry):
        rows = pl.ds(pl.multiple_of(b * N, N), N)
        c_blk = cm[rows, :]
        for j in range(NP):
            at = lanes(j)
            state = sl[b, :, at] + pd[b, :, at] * entering[:, at]
            sl[b, :, at] = state
            high, low = halves(state)
            y[rows, at] = within[rows, at] + (dot(c_blk, high) + dot(c_blk, low)) * er[rows, at] + skip[:, at] * x[rows, at].astype(f32)
        return carry

    lax.fori_loop(0, NB, step, 0)


CH = 32


def norm(y, z, gain, normed):
    def step(i, carry):
        rows = pl.ds(pl.multiple_of(i * CH, CH), CH)
        z_val = z[rows, :].astype(f32)
        gated = y[rows, :] * (z_val / (1.0 + jnp.exp(-z_val)))
        factor = lax.rsqrt(jnp.mean(gated * gated, axis=1, keepdims=True) + 1e-05)
        normed[rows, :] = (gated * factor * gain[...]).astype(bf16)
        return carry

    lax.fori_loop(0, T // CH, step, 0)


def unnorm(y, within, x, z, gain, skip, d_normed, d_z, d_y):
    def step(i, carry):
        rows = pl.ds(pl.multiple_of(i * CH, CH), CH)
        z_val = z[rows, :].astype(f32)
        y_val = y[rows, :]
        sig = 1.0 / (1.0 + jnp.exp(-z_val))
        silu = z_val * sig
        gated = y_val * silu
        factor = lax.rsqrt(jnp.mean(gated * gated, axis=1, keepdims=True) + 1e-05)
        scaled = d_normed[rows, :] * gain[...]
        along = jnp.mean(scaled * gated, axis=1, keepdims=True)
        d_gated = factor * scaled - gated * (factor * factor * factor * along)
        d_z[rows, :] = (d_gated * y_val * (sig * (1.0 + z_val * (1.0 - sig)))).astype(bf16)
        d_mixed = d_gated * silu
        d_y[rows, :] = d_mixed
        own = within[rows, :]
        y[rows, :] = d_mixed * own
        d_normed[rows, :] = d_mixed * (y_val - skip[...] * x[rows, :].astype(f32) - own)
        return carry

    lax.fori_loop(0, T // CH, step, 0)


def gather_heads(work, sums):
    def step(b, carry):
        rows = pl.ds(pl.multiple_of(b * N, N), N)
        sums[:, rows] = head_sums(work[rows, :])
        return carry

    lax.fori_loop(0, NB, step, 0)


def state_grad(cm, r_t, keep_t, er, d_y, gl, qd, gt):
    gt[...] = jnp.zeros_like(gt)
    qd[NB - 1] = jnp.ones((1, HP), f32)

    def step(i, carry):
        b = NB - 1 - i
        base = pl.multiple_of(b * N, N)
        rows = pl.ds(base, N)
        c_flip = cm[rows, :].astype(f32).T.astype(bf16)
        for j in range(NP):
            at = lanes(j)
            last = pair_of(r_t, pl.ds(base + N - 1, 1), j, 1)[0]
            keep = pair_of(keep_t.at[b], slice(0, 1), j, 1)[0]
            high, low = halves(er[rows, at] * d_y[rows, at])
            grad = gt[:, at]
            gl[b, :, at] = grad
            decay = jnp.exp(last)
            gt[:, at] = keep * (decay * grad + dot(c_flip, high) + dot(c_flip, low))
            value = qd[b, :, at]

            @pl.when(b > 0)
            def _():
                qd[b - 1, :, at] = keep * decay * value

        return carry

    lax.fori_loop(0, NB, step, 0)


def backward_within(x, bm, cm, r, r_t, step_t, d_y, v, ds):
    def step(b, carry):
        rows = pl.ds(pl.multiple_of(b * N, N), N)
        mask = iota((N, N), 0) <= iota((N, N), 1)
        scores = dot(bm[rows, :], cm[rows, :], NT)
        total = jnp.zeros((N, N), f32)
        for j in range(NP):
            at = lanes(j)
            run0 = jnp.broadcast_to(r_t[rows, 2 * j : 2 * j + 1], (N, N))
            run1 = jnp.broadcast_to(r_t[rows, 2 * j + 1 : 2 * j + 2], (N, N))
            size = pair_of(step_t, rows, j, N)[0]
            decays = [
                jnp.exp(jnp.where(mask, r[2 * j + k : 2 * j + k + 1, rows] - col, OFF))
                for k, col in enumerate((run0, run1))
            ]
            high, low = halves(d_y[rows, at])
            mixing = jnp.concatenate([(decay * scores).astype(bf16) for decay in decays], axis=1)
            v[rows, at] = dot(mixing, stacked(high)) + dot(mixing, stacked(low))
            sized = (x[rows, at].astype(f32) * size).astype(bf16)
            both = stacked(sized)
            product = dot(both, high, NT) + dot(both, low, NT)
            total = total + product[:N] * decays[0] + product[N:] * decays[1]
        ds[b] = total.astype(bf16)
        return carry

    lax.fori_loop(0, NB, step, 0)


def backward_rest(span, x, bm, cm, r_t, step_t, skip, d_y, v, ds, xw, er, sl, gl, qd, arriving, ge, gy, psi, own, d_x, d_b, d_c):
    def step(b, carry):
        base = pl.multiple_of(b * N, N)
        rows = pl.ds(base, N)
        b_blk, c_blk = bm[rows, :], cm[rows, :]
        for j in range(NP):
            at = lanes(j)
            run = pair_of(r_t, rows, j, N)[0]
            size = pair_of(step_t, rows, j, N)[0]
            last = pair_of(r_t, pl.ds(base + N - 1, 1), j, 1)[0]
            grad = gl[b, :, at] + qd[b, :, at] * arriving[:, at]
            passing = grad * sl[b, :, at]
            psi[b, :, at] = jnp.exp(last) * jnp.sum(passing.reshape(N // 8, 8, N), axis=0)
            high, low = halves(grad)
            ge[0, :, at] = high
            ge[1, :, at] = low
            local = v[rows, at]
            gy[0, :, at], gy[1, :, at] = halves(er[rows, at] * d_y[rows, at])
            reach = dot(b_blk, high) + dot(b_blk, low)
            carried = jnp.exp(last - run) * reach
            x_val = x[rows, at].astype(f32)
            sized = x_val * size
            d_x[rows, at] = (size * (local + carried) + skip[:, at] * d_y[rows, at]).astype(bf16)
            own[rows, at] = sized.astype(bf16).astype(f32) * local
            v[rows, at] = xw[rows, at].astype(f32) * reach
            d_y[rows, at] = x_val * (local + carried)
        d_b[rows, :] = (dot(ds[b], c_blk) + dot(xw[rows, :], ge[0], NT) + dot(xw[rows, :], ge[1], NT)).astype(bf16)
        late = sl[b].astype(bf16)
        d_c[rows, :] = (dot(ds[b], b_blk, TN) + dot(gy[0], late, NT) + dot(gy[1], late, NT)).astype(bf16)
        return carry

    lax.fori_loop(*span, step, 0)


def steps_grad(dt, bias, alog, step, psi, row_own, row_carried, own, carried, whole, out):
    row, col = iota((N, N), 0), iota((N, N), 1)
    since = (row >= col).astype(f32)
    before = (row < col).astype(f32)
    raw = dt[...] + column(bias)
    sig = 1.0 / (1.0 + jnp.exp(-raw))
    pull = jnp.exp(column(alog))
    ones = head_rows().astype(f32)
    for b in range(NB):
        at = lanes(b)
        past = jnp.sum(dot(ones, psi[b], NT, HI), axis=1, keepdims=True)
        d_rate = dot(row_own[:, at] - own[:, at] + row_carried[:, at], since, precision=HI) + past
        d_rate = d_rate + dot(carried[:, at], before, precision=HI)
        out[:, at] = (whole[:, at] - pull * d_rate) * sig[:, at]


MESH = pl.DeviceIdType.MESH
SHARD = 128
HALF = HP // 2
D = 4096


def mod(value, size):
    return lax.rem(value + size, size)


def greet(me, heads):
    barrier = pltpu.get_barrier_semaphore()

    def step(k, carry):
        pl.semaphore_signal(barrier, inc=1, device_id={"seq": lax.rem(me + k, SEQ)}, device_id_type=MESH)
        return carry

    lax.fori_loop(1, SEQ, step, 0)
    for h in heads:
        pl.semaphore_signal(barrier, inc=1, device_id={"head": h}, device_id_type=MESH)
    pl.semaphore_wait(barrier, SEQ - 1 + len(heads))


def remote(src, dst, ssem, rsem, **device):
    return pltpu.make_async_remote_copy(
        src_ref=src, dst_ref=dst, send_sem=ssem, recv_sem=rsem, device_id=device, device_id_type=MESH
    )


SLICE = 32


def each_other(me, fn):
    def step(k, carry):
        fn(lax.rem(me + k, SEQ))
        return carry

    lax.fori_loop(1, SEQ, step, 0)


def to_copy(me, rows, buf, land, ssem, rsem, other):
    return remote(buf.at[other, :rows], land.at[me, :rows], ssem.at[other], rsem.at[me], seq=other)


def from_copy(me, rows, buf, land, ssem, rsem, other):
    return remote(buf.at[me, :rows], land.at[other, :rows], ssem.at[me], rsem.at[other], seq=other)


def exchange_out(me, state, decay, out1, in1, s1, r1):
    rows = SLICE if decay is None else SLICE + 8
    for j in range(NP):
        for i in range(N // SLICE):
            k = j * (N // SLICE) + i
            out1[k, :SLICE] = state[SLICE * i : SLICE * (i + 1), lanes(j)]
            if decay is not None:
                out1[k, SLICE:] = jnp.broadcast_to(decay[:, lanes(j)], (8, N))
    each_other(me, lambda o: to_copy(me, rows, out1, in1, s1, r1, o).start())
    in1[me, :rows] = out1[me, :rows]


def exchange_fold(me, backward, out1, in1, s1, r1, out2, in2, s2, r2):
    rows = SLICE if backward else SLICE + 8
    each_other(me, lambda o: from_copy(me, rows, out1, in1, s1, r1, o).wait_recv())

    def step(i, total):
        at = SEQ - 1 - i if backward else i
        out2[at] = total
        return total * in1[at, SLICE : SLICE + 1] + in1[at, :SLICE]

    lax.fori_loop(0, SEQ, step, jnp.zeros((SLICE, N), f32))
    each_other(me, lambda o: to_copy(me, SLICE, out2, in2, s2, r2, o).start())
    in2[me] = out2[me]


def exchange_in(me, backward, result, out1, in1, s1, r1, out2, in2, s2, r2):
    rows = SLICE if backward else SLICE + 8
    each_other(me, lambda o: from_copy(me, SLICE, out2, in2, s2, r2, o).wait_recv())
    for j in range(NP):
        for i in range(N // SLICE):
            result[SLICE * i : SLICE * (i + 1), lanes(j)] = in2[j * (N // SLICE) + i]

    def done(o):
        to_copy(me, rows, out1, in1, s1, r1, o).wait_send()
        to_copy(me, SLICE, out2, in2, s2, r2, o).wait_send()

    each_other(me, done)


EXCHANGE = [
    pltpu.VMEM((SEQ, SLICE + 8, N), f32),
    pltpu.VMEM((SEQ, SLICE + 8, N), f32),
    pltpu.SemaphoreType.DMA((SEQ,)),
    pltpu.SemaphoreType.DMA((SEQ,)),
    pltpu.VMEM((SEQ, SLICE, N), f32),
    pltpu.VMEM((SEQ, SLICE, N), f32),
    pltpu.SemaphoreType.DMA((SEQ,)),
    pltpu.SemaphoreType.DMA((SEQ,)),
]


class Torus:
    def __init__(self, half):
        self.half = half
        me = lax.axis_index("seq")
        x, y = lax.rem(me, 4), lax.rem(lax.div(me, 4), 4)
        self.z = lax.div(me, 16)
        self.p, self.q = (x, y) if half == 0 else (y, x)

    def at(self, z, p, q):
        return z * 16 + (q * 4 + p if self.half == 0 else p * 4 + q)

    def place(self, dz=0, dp=0, dq=0):
        z = 1 - self.z if dz else self.z
        return self.at(z, mod(self.p + dp, 4), mod(self.q + dq, 4))


class Gather:
    def __init__(self, half, buf, ssem, rsem):
        self.t, self.half, self.buf, self.ssem, self.rsem, self.n = Torus(half), half, buf, ssem, rsem, 0
        self.sent = []

    def copy(self, shard, to, index):
        ref = self.buf.at[self.half, shard]
        return remote(ref, ref, self.ssem.at[self.half, index], self.rsem.at[self.half, shard], seq=to)

    def send(self, shard, to):
        copy = self.copy(shard, to, self.n)
        copy.start()
        self.sent.append(copy)
        self.n += 1

    def wait(self, shard):
        self.copy(shard, self.t.place(dz=1), 0).wait_recv()

    def spread(self, shard):
        self.send(shard, self.t.place(dq=1))
        self.send(shard, self.t.place(dq=-1))

    def own(self):
        t = self.t
        mine = t.place()
        self.send(mine, t.place(dz=1))
        self.send(mine, t.place(dp=1))
        self.send(mine, t.place(dp=-1))
        self.spread(mine)

    def across(self):
        t = self.t
        other = t.place(dz=1)
        self.wait(other)
        self.send(other, t.place(dp=1))
        self.send(other, t.place(dp=-1))
        self.spread(other)

    def near(self):
        t = self.t
        for z in (0, 1):
            for dp in (-1, 1):
                shard = t.at(z, mod(t.p + dp, 4), t.q)
                self.wait(shard)
                if (z, dp) in ((0, -1), (1, 1)):
                    self.send(shard, t.place(dp=-dp))
                self.spread(shard)

    def far(self):
        t = self.t
        for z in (0, 1):
            shard = t.at(z, mod(t.p + 2, 4), t.q)
            self.wait(shard)
            self.spread(shard)

    def pass_on(self, ks):
        t = self.t
        for k in ks:
            p = mod(t.p + (0, 1, 3, 2)[k], 4)
            for z, dq in ((0, -1), (1, 1)):
                shard = t.at(z, p, mod(t.q + dq, 4))
                self.wait(shard)
                self.send(shard, t.place(dq=-dq))

    def rest(self, ends):
        t = self.t
        for p in range(4):
            for z, dq in ends:
                self.wait(t.at(z, p, mod(t.q + dq, 4)))

    def multiply(self, cots, out, dqs, first):
        t = self.t
        at = slice(HALF * self.half, HALF * (self.half + 1))
        total = None if first else out[:, at]
        for dq in dqs:
            for p in range(4):
                pair = [t.at(z, p, mod(t.q + dq, 4)) for z in (0, 1)]
                left = [
                    cots[lax.div(k, 8), :, pl.ds(pl.multiple_of(lax.rem(k, 8) * SHARD, SHARD), SHARD)] for k in pair
                ]
                right = [self.buf[self.half, k] for k in pair]
                term = dot(jnp.concatenate(left, axis=1), jnp.concatenate(right, axis=0))
                total = term if total is None else total + term
        out[:, at] = total

    def close(self):
        for copy in self.sent:
            copy.wait_send()


class Heads:
    PARTS = 2

    def __init__(self, buf, ssem, rsem):
        self.h = lax.axis_index("head")
        self.core = self.h + 1 - 2 * lax.rem(self.h, 2)
        self.chip = lax.rem(self.h + 2, 4)
        self.buf, self.ssem, self.rsem, self.sent = buf, ssem, rsem, []

    def copy(self, block, part, to, index):
        ref = self.buf.at[block, pl.ds(part * (T // self.PARTS), T // self.PARTS)]
        return remote(ref, ref, self.ssem.at[index], self.rsem.at[block, part], head=to)

    def send(self, block, part, to):
        copy = self.copy(block, part, to, len(self.sent))
        copy.start()
        self.sent.append(copy)

    def own(self):
        for part in range(self.PARTS):
            self.send(self.h, part, self.chip)
        for part in range(self.PARTS):
            self.send(self.h, part, self.core)

    def across(self):
        for part in range(self.PARTS):
            self.copy(self.chip, part, self.chip, 0).wait_recv()
            self.send(self.chip, part, self.core)

    def rest(self):
        for part in range(self.PARTS):
            self.copy(self.core, part, self.core, 0).wait_recv()
            self.copy(lax.rem(self.core + 2, 4), part, self.core, 0).wait_recv()

    def close(self):
        for copy in self.sent:
            copy.wait_send()


FARP, FARM, NEARP, NEARM, PFARP, PFARM, PNEARP, PNEARM, ACROSS = 0, 4, 8, 16, 24, 25, 26, 28, 30
SLOTS = 31


class Scatter:
    def __init__(self, half, part, out, inn, ssem, rsem, acc, result):
        self.t, self.half, self.part, self.out, self.inn = Torus(half), half, part, out, inn
        self.ssem, self.rsem, self.acc, self.result = ssem, rsem, acc, result

    def copy(self, slot, to):
        h = self.half
        return remote(self.out.at[h, slot], self.inn.at[h, slot], self.ssem.at[h, slot], self.rsem.at[h, slot], seq=to)

    def send(self, slot, value, to):
        self.out[self.half, slot] = value.astype(bf16)
        self.copy(slot, to).start()

    def got(self, slot):
        self.copy(slot, self.t.place(dz=1)).wait_recv()
        return self.inn[self.half, slot].astype(f32)

    def loop(self, fn):
        def step(i, carry):
            fn(lax.rem(self.t.p + 2 + 3 * i + 3 * lax.div(i * (i - 1), 2), 4))
            return carry

        lax.fori_loop(0, 4, step, 0)

    def q_far(self):
        t = self.t
        far = mod(t.q + 2, 4)

        def fn(p):
            self.send(FARP + p, self.part(self.half, t.at(0, p, far)), t.place(dq=1))
            self.send(FARM + p, self.part(self.half, t.at(1, p, far)), t.place(dq=-1))

        self.loop(fn)

    def q_near(self):
        t = self.t
        up, down = mod(t.q + 1, 4), mod(t.q - 1, 4)

        def fn(p):
            self.send(NEARP + 4 + p, self.part(self.half, t.at(1, p, up)), t.place(dq=1))
            self.send(NEARM + p, self.part(self.half, t.at(0, p, down)), t.place(dq=-1))

        self.loop(fn)

    def q_pass(self):
        t = self.t
        up, down = mod(t.q + 1, 4), mod(t.q - 1, 4)

        def fn(p):
            self.send(NEARP + p, self.part(self.half, t.at(0, p, up)) + self.got(FARP + p), t.place(dq=1))
            self.send(NEARM + 4 + p, self.part(self.half, t.at(1, p, down)) + self.got(FARM + p), t.place(dq=-1))

        self.loop(fn)

    def q_own(self):
        t = self.t

        def fn(p):
            for z in (0, 1):
                self.acc[self.half, z, p] = self.part(self.half, t.at(z, p, t.q))

        self.loop(fn)

    def total(self, z, p):
        return self.acc[self.half, z, p] + self.got(NEARP + 4 * z + p) + self.got(NEARM + 4 * z + p)

    def p_far(self):
        t = self.t
        far = mod(t.p + 2, 4)
        self.send(PFARP, self.total(0, far), t.place(dp=1))
        self.send(PFARM, self.total(1, far), t.place(dp=-1))

    def p_near(self):
        t = self.t
        up, down = mod(t.p + 1, 4), mod(t.p - 1, 4)
        self.send(PNEARP + 1, self.total(1, up), t.place(dp=1))
        self.send(PNEARM, self.total(0, down), t.place(dp=-1))
        self.send(PNEARP, self.total(0, up) + self.got(PFARP), t.place(dp=1))
        self.send(PNEARM + 1, self.total(1, down) + self.got(PFARM), t.place(dp=-1))

    def p_own(self):
        t = self.t
        for z in (0, 1):
            self.acc[self.half, z, t.p] = self.total(z, t.p)

    def p_sum(self, z):
        return self.acc[self.half, z, self.t.p] + self.got_at(PNEARP, z) + self.got_at(PNEARM, z)

    def got_at(self, base, z):
        return self.got(base + z)

    def z_out(self):
        t = self.t
        self.send(ACROSS, self.p_sum(1 - t.z), t.place(dz=1))

    def z_in(self):
        t = self.t
        self.result[:, HALF * self.half : HALF * (self.half + 1)] = self.p_sum(t.z) + self.got(ACROSS)

    def close(self):
        def step(slot, carry):
            self.copy(slot, self.t.place(dz=1)).wait_send()
            return carry

        lax.fori_loop(0, SLOTS, step, 0)


V = pltpu.VMEM
DMA = pltpu.SemaphoreType.DMA

SCRATCH = {
    "step": V((H, T), f32), "r": V((H, T), f32), "step_t": V((T, H), f32), "r_t": V((T, H), f32),
    "keep_t": V((NB, 1, H), f32), "skips": V((1, HP), f32),
    "within": V((T, HP), f32), "er": V((T, HP), f32), "xw": V((T, HP), bf16),
    "sl": V((NB + 1, N, HP), f32), "pd": V((NB + 1, 1, HP), f32), "st": V((N, HP), f32),
    "y": V((T, HP), f32), "normed": V((T, HP), bf16), "dn": V((T, HP), f32), "d_y": V((T, HP), f32),
    "row_own": V((H, T), f32), "row_carried": V((H, T), f32), "s1": V((H, T), f32), "s2": V((H, T), f32), "s3": V((H, T), f32),
    "gl": V((NB, N, HP), f32), "qd": V((NB, 1, HP), f32),
    "entering": V((N, HP), f32),
    "ds": V((NB, N, N), bf16), "ge": V((2, N, HP), bf16), "gy": V((2, N, HP), bf16), "psi": V((NB, 8, HP), f32),
    "wbuf": V((2, SEQ, SHARD, HALF), bf16), "cbuf": V((4, T, HP), bf16),
    "ws": DMA((2, 31)), "wr": DMA((2, SEQ)), "cs": DMA((6,)), "cr": DMA((4, 2)), "local": DMA((3,)),
    "out": V((2, SLOTS, SHARD, HALF), bf16), "inn": V((2, SLOTS, SHARD, HALF), bf16),
    "ss": DMA((2, SLOTS)), "rs": DMA((2, SLOTS)), "acc": V((2, 2, 4, SHARD, HALF), f32),
}


def kernel(x, z, bm, cm, dt, bias, alog, skip, gain, resets, w, cot, d_x, d_z, d_b, d_c, d_dt, d_w, *refs):
    count = len(SCRATCH)
    s = dict(zip(SCRATCH, refs[:count]))
    swap = refs[count:]
    me = lax.axis_index("seq")
    step, r, step_t, r_t, keep_t, skips = (s[k] for k in ("step", "r", "step_t", "r_t", "keep_t", "skips"))
    within, er, xw, sl, pd, st, y = (s[k] for k in ("within", "er", "xw", "sl", "pd", "st", "y"))
    normed, dn, d_y, gl, qd = (s[k] for k in ("normed", "dn", "d_y", "gl", "qd"))
    entering, cbuf, wbuf, gt = s["entering"], s["cbuf"], s["wbuf"], st

    heads = Heads(cbuf, s["cs"], s["cr"])
    gathers = [Gather(h, wbuf, s["ws"], s["wr"]) for h in (0, 1)]

    def part(half, shard):
        block, at = lax.div(shard, 8), lax.rem(shard, 8)
        cols = pl.ds(pl.multiple_of(at * SHARD, SHARD), SHARD)
        return dot(cbuf[block, :, cols], normed[:, HALF * half : HALF * (half + 1)], TN)

    scatters = [Scatter(h, part, s["out"], s["inn"], s["ss"], s["rs"], s["acc"], d_w) for h in (0, 1)]

    def gather(name, *args):
        for g in gathers:
            getattr(g, name)(*args)

    def scatter(*names):
        for name in names:
            for g in scatters:
                getattr(g, name)()

    def block(b):
        forward_block(b, x, bm, cm, r, r_t, step_t, keep_t, within, er, xw, sl, pd, st)

    local = s["local"]
    mine = [pltpu.make_async_copy(w.at[:, pl.ds(HALF * h, HALF)], wbuf.at[h, me], local.at[h]) for h in (0, 1)]
    mine.append(pltpu.make_async_copy(cot, cbuf.at[heads.h], local.at[2]))
    for copy in mine:
        copy.start()
    greet(me, [heads.core, heads.chip])
    for copy in mine:
        copy.wait()

    gather("own")
    heads.own()
    prepare(dt, bias, alog, resets, skip, step, r, step_t, r_t, keep_t, skips)
    forward_start(pd, st)
    block(0)
    gather("across")
    block(1)
    gather("near")
    block(2)
    block(3)
    sl[NB] = st[...]
    exchange_out(me, st, pd[NB], *swap[:4])
    gather("far")
    gather("pass_on", (0,))
    heads.across()
    exchange_fold(me, False, *swap)
    gather("pass_on", (1,))
    gather("pass_on", (2,))
    heads.rest()
    gather("multiply", cbuf, dn, (0,), True)
    gather("pass_on", (3,))
    exchange_in(me, False, entering, *swap)
    enter(x, cm, sl, pd, entering, er, skips, within, y)
    norm(y, z, gain, normed)
    scatter("q_far")
    gather("rest", ((1, -1), (0, 1)))
    gather("multiply", cbuf, dn, (1, 3), False)
    scatter("q_near")
    gather("rest", ((0, 2), (1, 2)))
    gather("multiply", cbuf, dn, (2,), False)
    unnorm(y, within, x, z, gain, skips, dn, d_z, d_y)
    state_grad(cm, r_t, keep_t, er, d_y, gl, qd, gt)
    exchange_out(me, gt, None, *swap[:4])
    scatter("q_pass")
    gather_heads(dn, s["row_carried"])
    scatter("q_own")
    backward_within(x, bm, cm, r, r_t, step_t, d_y, dn, s["ds"])
    exchange_fold(me, True, *swap)
    scatter("p_far")
    gather_heads(y, s["row_own"])
    scatter("p_near")
    exchange_in(me, True, entering, *swap)
    late = (x, bm, cm, r_t, step_t, skips, d_y, dn, s["ds"], xw, er, sl, gl, qd, entering, s["ge"], s["gy"], s["psi"], y, d_x, d_b, d_c)
    backward_rest((0, 2), *late)
    scatter("p_own", "z_out")
    backward_rest((2, 4), *late)
    gather_heads(y, s["s1"])
    gather_heads(dn, s["s2"])
    gather_heads(d_y, s["s3"])
    steps_grad(dt, bias, alog, step, s["psi"], s["row_own"], s["row_carried"], s["s1"], s["s2"], s["s3"], d_dt)
    scatter("z_in", "close")
    gather("close")
    heads.close()


def finish(*refs):
    half = len(refs) // 2
    for source, target in zip(refs[:half], refs[half:]):
        target[...] = source[...]


def body(x, z, bm, cm, dt, bias, alog, skip, gain, resets, w, cot):
    outs = [((T, HP), bf16), ((T, HP), bf16), ((T, N), bf16), ((T, N), bf16), ((H, T), f32), ((SHARD, HP), f32)]
    vmem = pl.BlockSpec(memory_space=pltpu.VMEM)
    results = pl.pallas_call(
        kernel,
        out_shape=[jax.ShapeDtypeStruct(shape, kind) for shape, kind in outs],
        in_specs=[vmem] * 10 + [pl.BlockSpec(memory_space=pl.ANY)] * 2,
        out_specs=[vmem] * len(outs),
        scratch_shapes=list(SCRATCH.values()) + EXCHANGE,
        compiler_params=pltpu.CompilerParams(vmem_limit_bytes=63 << 20, collective_id=0, has_side_effects=True),
    )(x, z, bm, cm, dt, bias[None], alog[None], skip[None], gain[None], resets, w, cot)
    blocks = [pl.BlockSpec((shape[0] // 4, shape[1]), lambda i: (i, 0)) for shape, kind in outs]
    blocks[4] = pl.BlockSpec((H, T // 4), lambda i: (0, i))
    return pl.pallas_call(
        finish,
        grid=(4,),
        out_shape=[jax.ShapeDtypeStruct(shape, kind) for shape, kind in outs],
        in_specs=blocks,
        out_specs=blocks,
    )(*results)


def solution(mesh):
    s, h = P("seq", "head"), P("head")
    return jax.shard_map(
        body,
        mesh=mesh,
        in_specs=(s, s, s, s, P("head", "seq"), h, h, h, h, P("head", "seq"), s, s),
        out_specs=(s, s, s, s, P("head", "seq"), s),
        check_vma=False,
    )
```

```python
import jax
import jax.numpy as jnp
from jax import lax
from jax.experimental import pallas as pl
from jax.experimental.pallas import tpu as pltpu
from jax.sharding import PartitionSpec as P

T = 512
N = 128
HP = 1024
H = 16
NB = T // N
NP = HP // N
SEQ = 32

f32 = jnp.float32
bf16 = jnp.bfloat16
HI = lax.Precision.HIGHEST
NN = (((1,), (0,)), ((), ()))
NT = (((1,), (1,)), ((), ()))
TN = (((0,), (0,)), ((), ()))
OFF = -1e30


def dot(a, b, dims=NN, precision=None):
    return lax.dot_general(a, b, dims, precision=precision, preferred_element_type=f32)


def iota(shape, axis):
    return lax.broadcasted_iota(jnp.int32, shape, axis)


def pair_of(ref, rows, j, count):
    first = jnp.broadcast_to(ref[rows, 2 * j : 2 * j + 1], (count, N))
    second = jnp.broadcast_to(ref[rows, 2 * j + 1 : 2 * j + 2], (count, N))
    return jnp.where(iota((count, N), 1) < 64, first, second), first, second


def head_rows():
    row, col = iota((H, HP), 0), iota((H, HP), 1)
    return ((col >= 64 * row) & (col < 64 * row + 64)).astype(bf16)


def halves(value):
    high = value.astype(bf16)
    return high, (value - high.astype(f32)).astype(bf16)


def head_sums(value):
    high, low = halves(value)
    ones = head_rows()
    return dot(ones, high, NT) + dot(ones, low, NT)


def stacked(value):
    low = iota(value.shape, 1) < 64
    zero = jnp.zeros_like(value)
    return jnp.concatenate([jnp.where(low, value, zero), jnp.where(low, zero, value)], axis=0)


def lanes(j):
    return slice(N * j, N * j + N)


def column(ref):
    eye = iota((H, H), 0) == iota((H, H), 1)
    return jnp.sum(jnp.where(eye, jnp.broadcast_to(ref[...], (H, H)), 0.0), axis=1, keepdims=True)


def prepare(dt, bias, alog, resets, skip, step, r, step_t, r_t, keep_t, skips):
    raw = dt[...] + column(bias)
    step[...] = jnp.maximum(raw, 0.0) + jnp.log1p(jnp.exp(-jnp.abs(raw)))
    rate = -step[...] * jnp.exp(column(alog))
    keep = 1.0 - resets[...].astype(f32)
    square = iota((H, H), 0) == iota((H, H), 1)
    for b in range(NB):
        spread = jnp.where(square, jnp.broadcast_to(keep[:, b : b + 1], (H, H)), 0.0)
        keep_t[b] = jnp.sum(spread, axis=0, keepdims=True)
    for j in range(NP):
        skips[:, lanes(j)] = pair_of(skip, slice(0, 1), j, 1)[0]
    row, col = iota((N, N), 0), iota((N, N), 1)
    upper = (row <= col).astype(f32)
    eye = (row == col).astype(f32)
    for b in range(NB):
        at = lanes(b)
        r[:, at] = dot(rate[:, at], upper, precision=HI)
        r_t[at, :] = dot(eye, r[:, at], NT, HI)
        step_t[at, :] = dot(eye, step[:, at], NT, HI)


def forward_block(b, x, bm, cm, r, r_t, step_t, keep_t, within, er, xw, sl, pd, st):
    base = b * N
    rows = pl.ds(base, N)
    mask = iota((N, N), 0) >= iota((N, N), 1)
    b_blk, c_blk = bm[rows, :], cm[rows, :]
    b_flip = b_blk.astype(f32).T.astype(bf16)
    scores = dot(c_blk, b_blk, NT)
    for j in range(NP):
        at = lanes(j)
        run, run0, run1 = pair_of(r_t, rows, j, N)
        size = pair_of(step_t, rows, j, N)[0]
        last = pair_of(r_t, pl.ds(base + N - 1, 1), j, 1)[0]
        keep = pair_of(keep_t.at[b], slice(0, 1), j, 1)[0]
        mixing = [
            (jnp.exp(jnp.where(mask, col - r[2 * j + k : 2 * j + k + 1, rows], OFF)) * scores).astype(bf16)
            for k, col in enumerate((run0, run1))
        ]
        x_val = x[rows, at].astype(f32)
        sized = x_val * size
        within[rows, at] = dot(jnp.concatenate(mixing, axis=1), stacked(sized.astype(bf16)))
        er[rows, at] = jnp.exp(run)
        weighted = (sized * jnp.exp(last - run)).astype(bf16)
        xw[rows, at] = weighted
        state = st[:, at] * keep
        sl[b, :, at] = state
        span = pd[b, :, at] * keep
        pd[b, :, at] = span
        decay = jnp.exp(last)
        pd[b + 1, :, at] = span * decay
        st[:, at] = state * decay + dot(b_flip, weighted)


def forward_start(pd, st):
    st[...] = jnp.zeros_like(st)
    pd[0] = jnp.ones((1, HP), f32)


def enter(x, cm, sl, pd, entering, er, skip, within, y):
    def step(b, carry):
        rows = pl.ds(pl.multiple_of(b * N, N), N)
        c_blk = cm[rows, :]
        for j in range(NP):
            at = lanes(j)
            state = sl[b, :, at] + pd[b, :, at] * entering[:, at]
            sl[b, :, at] = state
            high, low = halves(state)
            y[rows, at] = within[rows, at] + (dot(c_blk, high) + dot(c_blk, low)) * er[rows, at] + skip[:, at] * x[rows, at].astype(f32)
        return carry

    lax.fori_loop(0, NB, step, 0)


CH = 32


def norm(y, z, gain, normed):
    def step(i, carry):
        rows = pl.ds(pl.multiple_of(i * CH, CH), CH)
        z_val = z[rows, :].astype(f32)
        gated = y[rows, :] * (z_val / (1.0 + jnp.exp(-z_val)))
        factor = lax.rsqrt(jnp.mean(gated * gated, axis=1, keepdims=True) + 1e-05)
        normed[rows, :] = (gated * factor * gain[...]).astype(bf16)
        return carry

    lax.fori_loop(0, T // CH, step, 0)


def unnorm(y, within, x, z, gain, skip, d_normed, d_z, d_y):
    def step(i, carry):
        rows = pl.ds(pl.multiple_of(i * CH, CH), CH)
        z_val = z[rows, :].astype(f32)
        y_val = y[rows, :]
        sig = 1.0 / (1.0 + jnp.exp(-z_val))
        silu = z_val * sig
        gated = y_val * silu
        factor = lax.rsqrt(jnp.mean(gated * gated, axis=1, keepdims=True) + 1e-05)
        scaled = d_normed[rows, :] * gain[...]
        along = jnp.mean(scaled * gated, axis=1, keepdims=True)
        d_gated = factor * scaled - gated * (factor * factor * factor * along)
        d_z[rows, :] = (d_gated * y_val * (sig * (1.0 + z_val * (1.0 - sig)))).astype(bf16)
        d_mixed = d_gated * silu
        d_y[rows, :] = d_mixed
        own = within[rows, :]
        y[rows, :] = d_mixed * own
        d_normed[rows, :] = d_mixed * (y_val - skip[...] * x[rows, :].astype(f32) - own)
        return carry

    lax.fori_loop(0, T // CH, step, 0)


def gather_heads(work, sums):
    def step(b, carry):
        rows = pl.ds(pl.multiple_of(b * N, N), N)
        sums[:, rows] = head_sums(work[rows, :])
        return carry

    lax.fori_loop(0, NB, step, 0)


def state_grad(cm, r_t, keep_t, er, d_y, gl, qd, gt):
    gt[...] = jnp.zeros_like(gt)
    qd[NB - 1] = jnp.ones((1, HP), f32)

    def step(i, carry):
        b = NB - 1 - i
        base = pl.multiple_of(b * N, N)
        rows = pl.ds(base, N)
        c_flip = cm[rows, :].astype(f32).T.astype(bf16)
        for j in range(NP):
            at = lanes(j)
            last = pair_of(r_t, pl.ds(base + N - 1, 1), j, 1)[0]
            keep = pair_of(keep_t.at[b], slice(0, 1), j, 1)[0]
            high, low = halves(er[rows, at] * d_y[rows, at])
            grad = gt[:, at]
            gl[b, :, at] = grad
            decay = jnp.exp(last)
            gt[:, at] = keep * (decay * grad + dot(c_flip, high) + dot(c_flip, low))
            value = qd[b, :, at]

            @pl.when(b > 0)
            def _():
                qd[b - 1, :, at] = keep * decay * value

        return carry

    lax.fori_loop(0, NB, step, 0)


def backward_within(x, bm, cm, r, r_t, step_t, d_y, v, ds):
    def step(b, carry):
        rows = pl.ds(pl.multiple_of(b * N, N), N)
        mask = iota((N, N), 0) <= iota((N, N), 1)
        scores = dot(bm[rows, :], cm[rows, :], NT)
        total = jnp.zeros((N, N), f32)
        for j in range(NP):
            at = lanes(j)
            run0 = jnp.broadcast_to(r_t[rows, 2 * j : 2 * j + 1], (N, N))
            run1 = jnp.broadcast_to(r_t[rows, 2 * j + 1 : 2 * j + 2], (N, N))
            size = pair_of(step_t, rows, j, N)[0]
            decays = [
                jnp.exp(jnp.where(mask, r[2 * j + k : 2 * j + k + 1, rows] - col, OFF))
                for k, col in enumerate((run0, run1))
            ]
            high, low = halves(d_y[rows, at])
            mixing = jnp.concatenate([(decay * scores).astype(bf16) for decay in decays], axis=1)
            v[rows, at] = dot(mixing, stacked(high)) + dot(mixing, stacked(low))
            sized = (x[rows, at].astype(f32) * size).astype(bf16)
            both = stacked(sized)
            product = dot(both, high, NT) + dot(both, low, NT)
            total = total + product[:N] * decays[0] + product[N:] * decays[1]
        ds[b] = total.astype(bf16)
        return carry

    lax.fori_loop(0, NB, step, 0)


def backward_rest(span, x, bm, cm, r_t, step_t, skip, d_y, v, ds, xw, er, sl, gl, qd, arriving, ge, gy, psi, own, d_x, d_b, d_c):
    def step(b, carry):
        base = pl.multiple_of(b * N, N)
        rows = pl.ds(base, N)
        b_blk, c_blk = bm[rows, :], cm[rows, :]
        for j in range(NP):
            at = lanes(j)
            run = pair_of(r_t, rows, j, N)[0]
            size = pair_of(step_t, rows, j, N)[0]
            last = pair_of(r_t, pl.ds(base + N - 1, 1), j, 1)[0]
            grad = gl[b, :, at] + qd[b, :, at] * arriving[:, at]
            passing = grad * sl[b, :, at]
            psi[b, :, at] = jnp.exp(last) * jnp.sum(passing.reshape(N // 8, 8, N), axis=0)
            high, low = halves(grad)
            ge[0, :, at] = high
            ge[1, :, at] = low
            local = v[rows, at]
            gy[0, :, at], gy[1, :, at] = halves(er[rows, at] * d_y[rows, at])
            reach = dot(b_blk, high) + dot(b_blk, low)
            carried = jnp.exp(last - run) * reach
            x_val = x[rows, at].astype(f32)
            sized = x_val * size
            d_x[rows, at] = (size * (local + carried) + skip[:, at] * d_y[rows, at]).astype(bf16)
            own[rows, at] = sized.astype(bf16).astype(f32) * local
            v[rows, at] = xw[rows, at].astype(f32) * reach
            d_y[rows, at] = x_val * (local + carried)
        d_b[rows, :] = (dot(ds[b], c_blk) + dot(xw[rows, :], ge[0], NT) + dot(xw[rows, :], ge[1], NT)).astype(bf16)
        late = sl[b].astype(bf16)
        d_c[rows, :] = (dot(ds[b], b_blk, TN) + dot(gy[0], late, NT) + dot(gy[1], late, NT)).astype(bf16)
        return carry

    lax.fori_loop(*span, step, 0)


def steps_grad(dt, bias, alog, step, psi, row_own, row_carried, own, carried, whole, out):
    row, col = iota((N, N), 0), iota((N, N), 1)
    since = (row >= col).astype(f32)
    before = (row < col).astype(f32)
    raw = dt[...] + column(bias)
    sig = 1.0 / (1.0 + jnp.exp(-raw))
    pull = jnp.exp(column(alog))
    ones = head_rows().astype(f32)
    for b in range(NB):
        at = lanes(b)
        past = jnp.sum(dot(ones, psi[b], NT, HI), axis=1, keepdims=True)
        d_rate = dot(row_own[:, at] - own[:, at] + row_carried[:, at], since, precision=HI) + past
        d_rate = d_rate + dot(carried[:, at], before, precision=HI)
        out[:, at] = (whole[:, at] - pull * d_rate) * sig[:, at]


MESH = pl.DeviceIdType.MESH
SHARD = 128
HALF = HP // 2
D = 4096


def mod(value, size):
    return lax.rem(value + size, size)


def greet(me, heads):
    barrier = pltpu.get_barrier_semaphore()

    def step(k, carry):
        pl.semaphore_signal(barrier, inc=1, device_id={"seq": lax.rem(me + k, SEQ)}, device_id_type=MESH)
        return carry

    lax.fori_loop(1, SEQ, step, 0)
    for h in heads:
        pl.semaphore_signal(barrier, inc=1, device_id={"head": h}, device_id_type=MESH)
    pl.semaphore_wait(barrier, SEQ - 1 + len(heads))


def remote(src, dst, ssem, rsem, **device):
    return pltpu.make_async_remote_copy(
        src_ref=src, dst_ref=dst, send_sem=ssem, recv_sem=rsem, device_id=device, device_id_type=MESH
    )


SLICE = 32


def each_other(me, fn):
    def step(k, carry):
        fn(lax.rem(me + k, SEQ))
        return carry

    lax.fori_loop(1, SEQ, step, 0)


def to_copy(me, rows, buf, land, ssem, rsem, other):
    return remote(buf.at[other, :rows], land.at[me, :rows], ssem.at[other], rsem.at[me], seq=other)


def from_copy(me, rows, buf, land, ssem, rsem, other):
    return remote(buf.at[me, :rows], land.at[other, :rows], ssem.at[me], rsem.at[other], seq=other)


def exchange_out(me, state, decay, out1, in1, s1, r1):
    rows = SLICE if decay is None else SLICE + 1
    for j in range(NP):
        for i in range(N // SLICE):
            k = j * (N // SLICE) + i
            out1[k, :SLICE] = state[SLICE * i : SLICE * (i + 1), lanes(j)]
            if decay is not None:
                out1[k, SLICE:] = jnp.broadcast_to(decay[:, lanes(j)], (8, N))
    each_other(me, lambda o: to_copy(me, rows, out1, in1, s1, r1, o).start())
    in1[me, :rows] = out1[me, :rows]


def exchange_fold(me, backward, out1, in1, s1, r1, out2, in2, s2, r2):
    rows = SLICE if backward else SLICE + 1
    each_other(me, lambda o: from_copy(me, rows, out1, in1, s1, r1, o).wait_recv())

    def step(i, total):
        at = SEQ - 1 - i if backward else i
        out2[at] = total
        return total * in1[at, SLICE : SLICE + 1] + in1[at, :SLICE]

    lax.fori_loop(0, SEQ, step, jnp.zeros((SLICE, N), f32))
    each_other(me, lambda o: to_copy(me, SLICE, out2, in2, s2, r2, o).start())
    in2[me] = out2[me]


def exchange_in(me, backward, result, out1, in1, s1, r1, out2, in2, s2, r2):
    rows = SLICE if backward else SLICE + 1
    each_other(me, lambda o: from_copy(me, SLICE, out2, in2, s2, r2, o).wait_recv())
    for j in range(NP):
        for i in range(N // SLICE):
            result[SLICE * i : SLICE * (i + 1), lanes(j)] = in2[j * (N // SLICE) + i]

    def done(o):
        to_copy(me, rows, out1, in1, s1, r1, o).wait_send()
        to_copy(me, SLICE, out2, in2, s2, r2, o).wait_send()

    each_other(me, done)


EXCHANGE = [
    pltpu.VMEM((SEQ, SLICE + 8, N), f32),
    pltpu.VMEM((SEQ, SLICE + 8, N), f32),
    pltpu.SemaphoreType.DMA((SEQ,)),
    pltpu.SemaphoreType.DMA((SEQ,)),
    pltpu.VMEM((SEQ, SLICE, N), f32),
    pltpu.VMEM((SEQ, SLICE, N), f32),
    pltpu.SemaphoreType.DMA((SEQ,)),
    pltpu.SemaphoreType.DMA((SEQ,)),
]


class Torus:
    def __init__(self, half):
        self.half = half
        me = lax.axis_index("seq")
        x, y = lax.rem(me, 4), lax.rem(lax.div(me, 4), 4)
        self.z = lax.div(me, 16)
        self.p, self.q = (x, y) if half == 0 else (y, x)

    def at(self, z, p, q):
        return z * 16 + (q * 4 + p if self.half == 0 else p * 4 + q)

    def place(self, dz=0, dp=0, dq=0):
        z = 1 - self.z if dz else self.z
        return self.at(z, mod(self.p + dp, 4), mod(self.q + dq, 4))


class Gather:
    def __init__(self, half, buf, ssem, rsem):
        self.t, self.half, self.buf, self.ssem, self.rsem, self.n = Torus(half), half, buf, ssem, rsem, 0
        self.sent = []

    def copy(self, shard, to, index):
        ref = self.buf.at[self.half, shard]
        return remote(ref, ref, self.ssem.at[self.half, index], self.rsem.at[self.half, shard], seq=to)

    def send(self, shard, to):
        copy = self.copy(shard, to, self.n)
        copy.start()
        self.sent.append(copy)
        self.n += 1

    def wait(self, shard):
        self.copy(shard, self.t.place(dz=1), 0).wait_recv()

    def spread(self, shard):
        self.send(shard, self.t.place(dq=1))
        self.send(shard, self.t.place(dq=-1))

    def own(self):
        t = self.t
        mine = t.place()
        self.send(mine, t.place(dz=1))
        self.send(mine, t.place(dp=1))
        self.send(mine, t.place(dp=-1))
        self.spread(mine)

    def across(self):
        t = self.t
        other = t.place(dz=1)
        self.wait(other)
        self.send(other, t.place(dp=1))
        self.send(other, t.place(dp=-1))
        self.spread(other)

    def near(self):
        t = self.t
        for z in (0, 1):
            for dp in (-1, 1):
                shard = t.at(z, mod(t.p + dp, 4), t.q)
                self.wait(shard)
                if (z, dp) in ((0, -1), (1, 1)):
                    self.send(shard, t.place(dp=-dp))
                self.spread(shard)

    def far(self):
        t = self.t
        for z in (0, 1):
            shard = t.at(z, mod(t.p + 2, 4), t.q)
            self.wait(shard)
            self.spread(shard)

    def pass_on(self, ks):
        t = self.t
        for k in ks:
            p = mod(t.p + (0, 1, 3, 2)[k], 4)
            for z, dq in ((0, -1), (1, 1)):
                shard = t.at(z, p, mod(t.q + dq, 4))
                self.wait(shard)
                self.send(shard, t.place(dq=-dq))

    def rest(self, ends):
        t = self.t
        for p in range(4):
            for z, dq in ends:
                self.wait(t.at(z, p, mod(t.q + dq, 4)))

    def multiply(self, cots, out, dqs, first):
        t = self.t
        at = slice(HALF * self.half, HALF * (self.half + 1))
        total = None if first else out[:, at]
        for dq in dqs:
            for p in range(4):
                pair = [t.at(z, p, mod(t.q + dq, 4)) for z in (0, 1)]
                left = [
                    cots[lax.div(k, 8), :, pl.ds(pl.multiple_of(lax.rem(k, 8) * SHARD, SHARD), SHARD)] for k in pair
                ]
                right = [self.buf[self.half, k] for k in pair]
                term = dot(jnp.concatenate(left, axis=1), jnp.concatenate(right, axis=0))
                total = term if total is None else total + term
        out[:, at] = total

    def close(self):
        for copy in self.sent:
            copy.wait_send()


class Heads:
    PARTS = 2

    def __init__(self, buf, ssem, rsem):
        self.h = lax.axis_index("head")
        self.core = self.h + 1 - 2 * lax.rem(self.h, 2)
        self.chip = lax.rem(self.h + 2, 4)
        self.buf, self.ssem, self.rsem, self.sent = buf, ssem, rsem, []

    def copy(self, block, part, to, index):
        ref = self.buf.at[block, pl.ds(part * (T // self.PARTS), T // self.PARTS)]
        return remote(ref, ref, self.ssem.at[index], self.rsem.at[block, part], head=to)

    def send(self, block, part, to):
        copy = self.copy(block, part, to, len(self.sent))
        copy.start()
        self.sent.append(copy)

    def own(self):
        for part in range(self.PARTS):
            self.send(self.h, part, self.chip)
        for part in range(self.PARTS):
            self.send(self.h, part, self.core)

    def across(self):
        for part in range(self.PARTS):
            self.copy(self.chip, part, self.chip, 0).wait_recv()
            self.send(self.chip, part, self.core)

    def rest(self):
        for part in range(self.PARTS):
            self.copy(self.core, part, self.core, 0).wait_recv()
            self.copy(lax.rem(self.core + 2, 4), part, self.core, 0).wait_recv()

    def close(self):
        for copy in self.sent:
            copy.wait_send()


FARP, FARM, NEARP, NEARM, PFARP, PFARM, PNEARP, PNEARM, ACROSS = 0, 4, 8, 16, 24, 25, 26, 28, 30
SLOTS = 31


class Scatter:
    def __init__(self, half, part, out, inn, ssem, rsem, acc, result):
        self.t, self.half, self.part, self.out, self.inn = Torus(half), half, part, out, inn
        self.ssem, self.rsem, self.acc, self.result = ssem, rsem, acc, result

    def copy(self, slot, to):
        h = self.half
        return remote(self.out.at[h, slot], self.inn.at[h, slot], self.ssem.at[h, slot], self.rsem.at[h, slot], seq=to)

    def send(self, slot, value, to):
        self.out[self.half, slot] = value.astype(bf16)
        self.copy(slot, to).start()

    def got(self, slot):
        self.copy(slot, self.t.place(dz=1)).wait_recv()
        return self.inn[self.half, slot].astype(f32)

    def loop(self, fn):
        def step(i, carry):
            fn(lax.rem(self.t.p + 2 + 3 * i + 3 * lax.div(i * (i - 1), 2), 4))
            return carry

        lax.fori_loop(0, 4, step, 0)

    def q_far(self):
        t = self.t
        far = mod(t.q + 2, 4)

        def fn(p):
            self.send(FARP + p, self.part(self.half, t.at(0, p, far)), t.place(dq=1))
            self.send(FARM + p, self.part(self.half, t.at(1, p, far)), t.place(dq=-1))

        self.loop(fn)

    def q_near(self):
        t = self.t
        up, down = mod(t.q + 1, 4), mod(t.q - 1, 4)

        def fn(p):
            self.send(NEARP + 4 + p, self.part(self.half, t.at(1, p, up)), t.place(dq=1))
            self.send(NEARM + p, self.part(self.half, t.at(0, p, down)), t.place(dq=-1))

        self.loop(fn)

    def q_pass(self):
        t = self.t
        up, down = mod(t.q + 1, 4), mod(t.q - 1, 4)

        def fn(p):
            self.send(NEARP + p, self.part(self.half, t.at(0, p, up)) + self.got(FARP + p), t.place(dq=1))
            self.send(NEARM + 4 + p, self.part(self.half, t.at(1, p, down)) + self.got(FARM + p), t.place(dq=-1))

        self.loop(fn)

    def q_own(self):
        t = self.t

        def fn(p):
            for z in (0, 1):
                self.acc[self.half, z, p] = self.part(self.half, t.at(z, p, t.q))

        self.loop(fn)

    def total(self, z, p):
        return self.acc[self.half, z, p] + self.got(NEARP + 4 * z + p) + self.got(NEARM + 4 * z + p)

    def p_far(self):
        t = self.t
        far = mod(t.p + 2, 4)
        self.send(PFARP, self.total(0, far), t.place(dp=1))
        self.send(PFARM, self.total(1, far), t.place(dp=-1))

    def p_near(self):
        t = self.t
        up, down = mod(t.p + 1, 4), mod(t.p - 1, 4)
        self.send(PNEARP + 1, self.total(1, up), t.place(dp=1))
        self.send(PNEARM, self.total(0, down), t.place(dp=-1))
        self.send(PNEARP, self.total(0, up) + self.got(PFARP), t.place(dp=1))
        self.send(PNEARM + 1, self.total(1, down) + self.got(PFARM), t.place(dp=-1))

    def p_own(self):
        t = self.t
        for z in (0, 1):
            self.acc[self.half, z, t.p] = self.total(z, t.p)

    def p_sum(self, z):
        return self.acc[self.half, z, self.t.p] + self.got_at(PNEARP, z) + self.got_at(PNEARM, z)

    def got_at(self, base, z):
        return self.got(base + z)

    def z_out(self):
        t = self.t
        self.send(ACROSS, self.p_sum(1 - t.z), t.place(dz=1))

    def z_in(self):
        t = self.t
        self.result[:, HALF * self.half : HALF * (self.half + 1)] = self.p_sum(t.z) + self.got(ACROSS)

    def close(self):
        def step(slot, carry):
            self.copy(slot, self.t.place(dz=1)).wait_send()
            return carry

        lax.fori_loop(0, SLOTS, step, 0)


V = pltpu.VMEM
DMA = pltpu.SemaphoreType.DMA

SCRATCH = {
    "step": V((H, T), f32), "r": V((H, T), f32), "step_t": V((T, H), f32), "r_t": V((T, H), f32),
    "keep_t": V((NB, 1, H), f32), "skips": V((1, HP), f32),
    "within": V((T, HP), f32), "er": V((T, HP), f32), "xw": V((T, HP), bf16),
    "sl": V((NB + 1, N, HP), f32), "pd": V((NB + 1, 1, HP), f32), "st": V((N, HP), f32),
    "y": V((T, HP), f32), "normed": V((T, HP), bf16), "dn": V((T, HP), f32), "d_y": V((T, HP), f32),
    "row_own": V((H, T), f32), "row_carried": V((H, T), f32), "s1": V((H, T), f32), "s2": V((H, T), f32), "s3": V((H, T), f32),
    "gl": V((NB, N, HP), f32), "qd": V((NB, 1, HP), f32),
    "entering": V((N, HP), f32),
    "ds": V((NB, N, N), bf16), "ge": V((2, N, HP), bf16), "gy": V((2, N, HP), bf16), "psi": V((NB, 8, HP), f32),
    "wbuf": V((2, SEQ, SHARD, HALF), bf16), "cbuf": V((4, T, HP), bf16),
    "ws": DMA((2, 31)), "wr": DMA((2, SEQ)), "cs": DMA((6,)), "cr": DMA((4, 2)), "local": DMA((3,)),
    "out": V((2, SLOTS, SHARD, HALF), bf16), "inn": V((2, SLOTS, SHARD, HALF), bf16),
    "ss": DMA((2, SLOTS)), "rs": DMA((2, SLOTS)), "acc": V((2, 2, 4, SHARD, HALF), f32),
}


def kernel(x, z, bm, cm, dt, bias, alog, skip, gain, resets, w, cot, d_x, d_z, d_b, d_c, d_dt, d_w, *refs):
    count = len(SCRATCH)
    s = dict(zip(SCRATCH, refs[:count]))
    swap = refs[count:]
    me = lax.axis_index("seq")
    step, r, step_t, r_t, keep_t, skips = (s[k] for k in ("step", "r", "step_t", "r_t", "keep_t", "skips"))
    within, er, xw, sl, pd, st, y = (s[k] for k in ("within", "er", "xw", "sl", "pd", "st", "y"))
    normed, dn, d_y, gl, qd = (s[k] for k in ("normed", "dn", "d_y", "gl", "qd"))
    entering, cbuf, wbuf, gt = s["entering"], s["cbuf"], s["wbuf"], st

    heads = Heads(cbuf, s["cs"], s["cr"])
    gathers = [Gather(h, wbuf, s["ws"], s["wr"]) for h in (0, 1)]

    def part(half, shard):
        block, at = lax.div(shard, 8), lax.rem(shard, 8)
        cols = pl.ds(pl.multiple_of(at * SHARD, SHARD), SHARD)
        return dot(cbuf[block, :, cols], normed[:, HALF * half : HALF * (half + 1)], TN)

    scatters = [Scatter(h, part, s["out"], s["inn"], s["ss"], s["rs"], s["acc"], d_w) for h in (0, 1)]

    def gather(name, *args):
        for g in gathers:
            getattr(g, name)(*args)

    def scatter(*names):
        for name in names:
            for g in scatters:
                getattr(g, name)()

    def block(b):
        forward_block(b, x, bm, cm, r, r_t, step_t, keep_t, within, er, xw, sl, pd, st)

    local = s["local"]
    mine = [pltpu.make_async_copy(w.at[:, pl.ds(HALF * h, HALF)], wbuf.at[h, me], local.at[h]) for h in (0, 1)]
    mine.append(pltpu.make_async_copy(cot, cbuf.at[heads.h], local.at[2]))
    for copy in mine:
        copy.start()
    greet(me, [heads.core, heads.chip])
    for copy in mine:
        copy.wait()

    gather("own")
    heads.own()
    prepare(dt, bias, alog, resets, skip, step, r, step_t, r_t, keep_t, skips)
    forward_start(pd, st)
    block(0)
    gather("across")
    block(1)
    gather("near")
    block(2)
    block(3)
    sl[NB] = st[...]
    exchange_out(me, st, pd[NB], *swap[:4])
    gather("far")
    gather("pass_on", (0,))
    heads.across()
    exchange_fold(me, False, *swap)
    gather("pass_on", (1,))
    gather("pass_on", (2,))
    heads.rest()
    gather("multiply", cbuf, dn, (0,), True)
    gather("pass_on", (3,))
    exchange_in(me, False, entering, *swap)
    enter(x, cm, sl, pd, entering, er, skips, within, y)
    norm(y, z, gain, normed)
    scatter("q_far")
    gather("rest", ((1, -1), (0, 1)))
    gather("multiply", cbuf, dn, (1, 3), False)
    scatter("q_near")
    gather("rest", ((0, 2), (1, 2)))
    gather("multiply", cbuf, dn, (2,), False)
    unnorm(y, within, x, z, gain, skips, dn, d_z, d_y)
    state_grad(cm, r_t, keep_t, er, d_y, gl, qd, gt)
    exchange_out(me, gt, None, *swap[:4])
    scatter("q_pass")
    gather_heads(dn, s["row_carried"])
    scatter("q_own")
    backward_within(x, bm, cm, r, r_t, step_t, d_y, dn, s["ds"])
    exchange_fold(me, True, *swap)
    scatter("p_far")
    gather_heads(y, s["row_own"])
    scatter("p_near")
    exchange_in(me, True, entering, *swap)
    late = (x, bm, cm, r_t, step_t, skips, d_y, dn, s["ds"], xw, er, sl, gl, qd, entering, s["ge"], s["gy"], s["psi"], y, d_x, d_b, d_c)
    backward_rest((0, 2), *late)
    scatter("p_own", "z_out")
    backward_rest((2, 4), *late)
    gather_heads(y, s["s1"])
    gather_heads(dn, s["s2"])
    gather_heads(d_y, s["s3"])
    steps_grad(dt, bias, alog, step, s["psi"], s["row_own"], s["row_carried"], s["s1"], s["s2"], s["s3"], d_dt)
    scatter("z_in", "close")
    gather("close")
    heads.close()


def finish(*refs):
    half = len(refs) // 2
    for source, target in zip(refs[:half], refs[half:]):
        target[...] = source[...]


def body(x, z, bm, cm, dt, bias, alog, skip, gain, resets, w, cot):
    outs = [((T, HP), bf16), ((T, HP), bf16), ((T, N), bf16), ((T, N), bf16), ((H, T), f32), ((SHARD, HP), f32)]
    vmem = pl.BlockSpec(memory_space=pltpu.VMEM)
    results = pl.pallas_call(
        kernel,
        out_shape=[jax.ShapeDtypeStruct(shape, kind) for shape, kind in outs],
        in_specs=[vmem] * 10 + [pl.BlockSpec(memory_space=pl.ANY)] * 2,
        out_specs=[vmem] * len(outs),
        scratch_shapes=list(SCRATCH.values()) + EXCHANGE,
        compiler_params=pltpu.CompilerParams(vmem_limit_bytes=63 << 20, collective_id=0, has_side_effects=True),
    )(x, z, bm, cm, dt, bias[None], alog[None], skip[None], gain[None], resets, w, cot)
    blocks = [pl.BlockSpec((shape[0] // 4, shape[1]), lambda i: (i, 0)) for shape, kind in outs]
    blocks[4] = pl.BlockSpec((H, T // 4), lambda i: (0, i))
    return pl.pallas_call(
        finish,
        grid=(4,),
        out_shape=[jax.ShapeDtypeStruct(shape, kind) for shape, kind in outs],
        in_specs=blocks,
        out_specs=blocks,
    )(*results)


def solution(mesh):
    s, h = P("seq", "head"), P("head")
    return jax.shard_map(
        body,
        mesh=mesh,
        in_specs=(s, s, s, s, P("head", "seq"), h, h, h, h, P("head", "seq"), s, s),
        out_specs=(s, s, s, s, P("head", "seq"), s),
        check_vma=False,
    )
```
